512 devices in a mesh: blk: 16 (over z_lo, y), seq: 32 (over x, z_hi, core).
Axes of the slice: x: 4, y: 8, z: 8 (z_hi: 4, z_lo: 2; z = z_hi * 2 + z_lo), core: 2. Of those that a mesh axis runs over, the one named last changes fastest.
Arguments:
- tokens: bfloat16 [16, 8192, 1024], P('blk', 'seq'), may hold values from -128 to 128
- expert_ids: int32 [16, 8192, 1], P('blk', 'seq'), may hold values from 0 to 31; in each aligned block of 256 rows (0 to 255, 256 to 511, ..., all dimensions but the last counted through in order) at most 16 rows name the same one
- expert_capacity: int32 [32], replicated, may hold values from 8 to 16, as said below
- kernel_weight: bfloat16 [1024, 496], replicated, may hold values from -1 to 1
- norm_gain: bfloat16 [1024], replicated, may hold values from 0.25 to 1.75
- router: bfloat16 [1024, 32], replicated, may hold values from -0.1875 to 0.1875
- expert_gate: bfloat16 [32, 1024, 2048], P('seq', None, 'blk'), may hold values from -0.1875 to 0.1875
- expert_up: bfloat16 [32, 1024, 2048], P('seq', None, 'blk'), may hold values from -0.1875 to 0.1875
- expert_down: bfloat16 [32, 1024, 2048], P('seq', None, 'blk'), may hold values from -0.125 to 0.125
Outputs:
- result: bfloat16 [16, 8192, 1024], P('blk', 'seq')
The draws below stay inside these ranges and needn't reach their ends.
Inputs may be any that keep to these rules, and one draw needn't show every extreme that they name: `expert_ids`: in each aligned block of 256 positions (the positions of one device) no expert is named more than 16 times, a bound that some block reaches. `expert_capacity`: some expert has capacity exactly 16.
All inputs are finite; a program needn't handle non-finite values.
Results may differ from the reference program's by a relative error of at most 0.004.
Values may be sent and summed in bfloat16 or wider, within the bound.
A program may use at most 128 MiB of HBM per device.

```python
import math
import jax
import jax.numpy as jnp
import numpy as np
from jax import lax

D = 1024
HEADS = 16
TAPS = 31
FF = 2048
TOK_DEV = 256
HEAD_DIM = 64
HALF = 15
SEQS = 16
LENGTH = 8192
EXPERTS = 32
CAP = 16
N_SEQ = 32


def kernel_base(key):
    values = jax.random.normal(jax.random.fold_in(key, 7), (D, HEADS * TAPS), jnp.float32)
    return jnp.clip(values, -5.0, 5.0) / math.sqrt(D)


def draw_kernel_weight(key, part):
    return kernel_base(key).astype(jnp.bfloat16)


def draw_expert_capacity(key, part):
    lower = max(1, CAP // 2)
    levels = jax.random.randint(jax.random.fold_in(key, 21), (EXPERTS,), lower, CAP + 1)
    which = jax.random.randint(jax.random.fold_in(key, 22), (), 0, EXPERTS)
    return jnp.where(jnp.arange(EXPERTS) == which, CAP, levels).astype(jnp.int32)


def draw_tokens(key, part):
    total = SEQS * LENGTH
    rows = jnp.clip(jax.random.normal(jax.random.fold_in(key, 17), (total, D), jnp.float32), -6.0, 6.0)
    return rows.reshape(SEQS, LENGTH, D).astype(jnp.bfloat16)


def shard_levels(key, shape, cuts, least, largest):
    loudness = 1.0
    for position, blocks in cuts:
        steps = jax.random.uniform(jax.random.fold_in(jax.random.fold_in(key, 6), position), (blocks,), jnp.float32, least / len(cuts), largest / len(cuts))
        loudness = loudness * jnp.repeat(jnp.exp(steps), shape[position] // blocks).reshape((-1,) + (1,) * (len(shape) - 1 - position))
    return loudness


def shared_out(own_key, own, number, rows, amount, top, most, slope):
    ranking = jax.random.permutation(own_key, amount)
    packed, usual = shares(amount, rows * top, most, slope, True), shares(amount, rows * top, most, slope, False)
    places = jnp.arange(amount)

    def named(tallies, offset_by):
        used = int((tallies > 0).sum())
        fixed = max(1, used // 4)
        moved = fixed + (places - fixed + offset_by * (used - fixed)) % max(1, amount - fixed)
        return jnp.zeros((amount,), jnp.int32).at[ranking[jnp.where(places < fixed, places, moved)]].set(jnp.asarray(tallies, jnp.int32))

    tallies = jnp.where(number % 4 == 0, named(packed, number // 4), named(usual, number - number // 4 - 1))
    mixed = jax.random.permutation(jax.random.fold_in(own, 3), amount)
    giver, sink = mixed[0:amount // 2 * 2:2], mixed[1:amount // 2 * 2:2]
    slack = jnp.minimum(tallies[giver] - 1, most - tallies[sink]) // 2
    slack = jnp.where((giver == ranking[0]) | (sink == ranking[0]) | (tallies[sink] == 0), 0, jnp.maximum(slack, 0))
    moved = jax.random.randint(jax.random.fold_in(own, 4), (amount // 2,), 0, 1 << 20) % (slack + 1)
    tallies = tallies.at[giver].add(-moved).at[sink].add(moved)
    items = jnp.searchsorted(jnp.cumsum(tallies), jnp.arange(rows * top), side="right").astype(jnp.int32)
    listing = items.reshape(top, rows).T
    listing = listing[jax.random.permutation(jax.random.fold_in(own, 1), rows)]
    offset_by = jax.random.randint(jax.random.fold_in(own, 2), (rows, 1), 0, top)
    return jnp.take_along_axis(listing, (jnp.arange(top)[None, :] + offset_by) % top, axis=1)


def shares(amount, total, bound, lean, full):
    loads = [(1 << 20) // math.isqrt(rank ** lean) + 1 for rank in range(1, amount + 1)]
    largest = bound if full else min(bound, max(-(-total // amount), total * loads[0] // sum(loads)))
    least = 1 if total - largest >= amount - 1 else 0
    holding, spare = [largest] + [least] * (amount - 1), total - largest - least * (amount - 1)
    while spare > 0:
        candidates = [i for i in range(1, amount) if holding[i] < largest] or [i for i in range(1, amount) if holding[i] < bound]
        whole, remaining = sum([loads[i] for i in candidates]), spare
        for i in candidates:
            extra = min(bound - holding[i], max(1, remaining * loads[i] // whole), spare)
            holding[i] = holding[i] + extra
            spare = spare - extra
    return np.array(holding)


def noise(key, extent, deviation, bound, cuts=(), held_as=jnp.bfloat16):
    level = shard_levels(key, extent, cuts, -0.22, 0.18) if cuts else 1.0
    values = jax.random.normal(key, extent, jnp.float32) * deviation * level
    return jnp.minimum(jnp.maximum(values, -bound), bound).astype(held_as)


def setup_inputs(seed: int = 0) -> dict:
    key_of = jax.random.split(jax.random.key(seed), 10)
    tokens = draw_tokens(jax.random.fold_in(key_of[9], 71), 0)
    expert_ids_keys = jax.random.split(jax.random.fold_in(key_of[1], 1), SEQS * LENGTH // TOK_DEV)
    expert_ids_turns = jax.random.permutation(jax.random.fold_in(key_of[1], 3), SEQS * LENGTH // TOK_DEV)
    expert_ids = jax.vmap(lambda own, number: shared_out(jax.random.fold_in(key_of[1], 2), own, number, TOK_DEV, EXPERTS, 1, CAP, 1))(expert_ids_keys, expert_ids_turns).reshape((SEQS, LENGTH, 1))
    expert_capacity = draw_expert_capacity(jax.random.fold_in(key_of[9], 71), 0)
    kernel_weight = draw_kernel_weight(jax.random.fold_in(key_of[9], 71), 0)
    norm_gain = jnp.clip(1.0 + 0.15 * jax.random.normal(key_of[4], (D,), jnp.float32), 0.25, 1.75).astype(jnp.bfloat16)
    router = noise(key_of[5], (D, EXPERTS), D ** -0.5, 0.1875)
    expert_gate = noise(key_of[6], (EXPERTS, D, FF), D ** -0.5, 0.1875, ((0, 32), (2, 16)))
    expert_up = noise(key_of[7], (EXPERTS, D, FF), D ** -0.5, 0.1875, ((0, 32), (2, 16)))
    expert_down = noise(key_of[8], (EXPERTS, D, FF), FF ** -0.5, 0.125, ((0, 32), (2, 16)))
    return dict(tokens=tokens, expert_ids=expert_ids, expert_capacity=expert_capacity, kernel_weight=kernel_weight, norm_gain=norm_gain, router=router, expert_gate=expert_gate, expert_up=expert_up, expert_down=expert_down)


EPS = 1e-06

def reference(tokens, expert_ids, expert_capacity, kernel_weight, norm_gain, router, expert_gate, expert_up, expert_down):
    flat = tokens.reshape(-1, D)
    logits = jnp.dot(flat, kernel_weight, preferred_element_type=jnp.float32).reshape(SEQS, LENGTH, HEADS, TAPS)
    probs = jax.nn.softmax(logits, axis=-1).astype(jnp.bfloat16)
    padded = jnp.pad(tokens, ((0, 0), (HALF, HALF), (0, 0)))
    mixed = tokens.astype(jnp.float32)
    for k in range(TAPS):
        weight = jnp.repeat(probs[:, :, :, k].astype(jnp.float32), HEAD_DIM, axis=2)
        mixed = mixed + weight * padded[:, k:k + LENGTH].astype(jnp.float32)
    scale = lax.rsqrt(lax.optimization_barrier(jnp.mean(mixed * mixed, axis=-1, keepdims=True)) + EPS)
    normed = (mixed * scale * norm_gain.astype(jnp.float32)).astype(jnp.bfloat16)
    blocks = SEQS * N_SEQ
    ids = expert_ids.reshape(blocks, TOK_DEV).astype(jnp.int32)
    onehot = (ids[:, :, None] == jnp.arange(EXPERTS, dtype=jnp.int32)[None, None, :]).astype(jnp.int32)
    rank = lax.optimization_barrier(jnp.sum((jnp.cumsum(onehot, axis=1) - 1) * onehot, axis=-1)).astype(jnp.int32)
    limit = expert_capacity[ids]
    kept = rank < limit
    gate_all = jnp.dot(normed.reshape(-1, D), router, preferred_element_type=jnp.float32)
    chosen = jnp.take_along_axis(gate_all, ids.reshape(-1, 1), axis=1).reshape(blocks, TOK_DEV)
    gate = jax.nn.sigmoid(chosen)
    slot = jnp.where(kept, ids * CAP + rank, EXPERTS * CAP).astype(jnp.int32)
    block_index = jnp.broadcast_to(jnp.arange(blocks, dtype=jnp.int32)[:, None], (blocks, TOK_DEV))
    normed_blocks = normed.reshape(blocks, TOK_DEV, D)
    buffer = jnp.zeros((blocks, EXPERTS * CAP + 1, D), jnp.bfloat16).at[block_index, slot].set(normed_blocks)
    buffer = buffer[:, :EXPERTS * CAP].reshape(blocks, EXPERTS, CAP, D)

    def expert_step(index):
        rows = buffer[:, index].reshape(-1, D)
        gated = jnp.dot(rows, expert_gate[index], preferred_element_type=jnp.float32)
        lifted = jnp.dot(rows, expert_up[index], preferred_element_type=jnp.float32)
        act = (jax.nn.silu(gated) * lifted).astype(jnp.bfloat16)
        output = lax.dot_general(act, expert_down[index], (((1,), (1,)), ((), ())), preferred_element_type=jnp.float32)
        return output.astype(jnp.bfloat16).reshape(blocks, CAP, D)
    outputs = lax.map(expert_step, jnp.arange(EXPERTS, dtype=jnp.int32))
    token_out = outputs[ids, block_index, jnp.minimum(rank, CAP - 1)].astype(jnp.float32)
    token_out = jnp.where(kept[:, :, None], token_out, jnp.float32(0.0))
    result = mixed.reshape(blocks, TOK_DEV, D) + gate[:, :, None] * token_out
    return result.astype(jnp.bfloat16).reshape(SEQS, LENGTH, D)
```

```python
import functools

import jax
import jax.numpy as jnp
from jax import lax
from jax.experimental import pallas as pl
from jax.experimental.pallas import tpu as pltpu
from jax.sharding import PartitionSpec as P

MESH = pl.DeviceIdType.MESH
F32 = jnp.float32
BF16 = jnp.bfloat16

D = 1024
HEADS = 16
TAPS = 31
HALF = 15
TOK = 256
EXPERTS = 32
CAP = 16
SLOTS = EXPERTS * CAP
EPS = 1e-06

NX, NH, NC, NY = 4, 4, 2, 8
GROUP = NX * NC * CAP
PIECE = 128
PARTS = 2
FEAT = D // PARTS

OWN, FAR = 0, 7
LEFT = (0, 1, 2, 3, 7)
RIGHT = (0, 4, 5, 6, 7)
ORDER = (0, 1, 4, 2, 5, 3, 6, 7)


def dot(a, b):
    return jnp.dot(a, b, preferred_element_type=F32)


def dot_nt(a, b):
    return lax.dot_general(a, b, (((1,), (1,)), ((), ())), preferred_element_type=F32)


def iota(shape, dim):
    return lax.broadcasted_iota(jnp.int32, shape, dim)


def layer(
    tokens, idc, idr, capc, capr, kwt, gain, router, gate_w, up_w, down_w,
    out,
    xp, pt, mixed, normed, packed, sel, gate_s,
    rows, gu, wd, act, ps, pr, mine, bs, bk,
    local_sem, halo_s, halo_r, ag_s, ag_r, fwd_s, fwd_r, ex_s, ex_r, px_s, px_r, ret_s, ret_r,
):
    s = lax.axis_index("seq")
    b = lax.axis_index("blk")
    lo, y = b // NY, lax.rem(b, NY)
    c = lax.rem(s, NC)
    h = lax.rem(s // NC, NH)
    x = s // (NC * NH)
    right = lo * NY + lax.rem(y + 1, NY)
    left = lo * NY + lax.rem(y + NY - 1, NY)
    pair = (1 - lo) * NY + y
    seqs = NX * NH * NC

    barrier = pltpu.get_barrier_semaphore()

    def greet(i, _):
        t = lax.rem(s + i, seqs)
        for other in range(2):
            pl.semaphore_signal(barrier, inc=1, device_id=(other * NY + y, t), device_id_type=MESH)
        return 0

    lax.fori_loop(1, seqs, greet, 0)
    for t in (pair, left, right):
        pl.semaphore_signal(barrier, inc=1, device_id=(t, s), device_id_type=MESH)
    pl.semaphore_wait(barrier, 2 * (seqs - 1) + 3)

    def remote(src, dst, ss, rs, blk, seq):
        return pltpu.make_async_remote_copy(
            src_ref=src, dst_ref=dst, send_sem=ss, recv_sem=rs, device_id=(blk, seq), device_id_type=MESH
        )

    def g_view(slot):
        return gu.at[slot, :, pl.ds(0, PIECE)]

    def u_view(slot):
        return gu.at[slot, :, pl.ds(PIECE, PIECE)]

    def d_view(slot):
        return wd.at[:, pl.ds(slot * PIECE, PIECE)]

    def d_half(slot, half):
        return wd.at[pl.ds(half * (D // 2), D // 2), pl.ds(slot * PIECE, PIECE)]

    views = (g_view, u_view, d_view)
    args = (gate_w.at[0], up_w.at[0], down_w.at[0])

    def hop(way, step, a):
        slots = (LEFT, RIGHT)[way]
        target = (right, left)[way]
        sems = ag_s.at[way, step - 1, a], ag_r.at[way, step - 1, a]
        if step == 4 and a == 2:
            src, dst = d_half(slots[3], way), d_half(FAR, way)
        elif step == 1:
            src, dst = args[a], views[a](slots[1])
        else:
            src, dst = views[a](slots[step - 1]), views[a](slots[step])
        return remote(src, dst, *sems, target, s)

    hops = []

    def send(step, a):
        for way in range(2):
            if step == 4 and a < 2 and a != way:
                continue
            cp = hop(way, step, a)
            cp.start()
            hops.append(cp)

    def forward(step, a):
        for way in range(2):
            hop(way, step, a).wait_recv()
            if step < 3 or a == 2 or a == way:
                cp = hop(way, step + 1, a)
                cp.start()
                hops.append(cp)

    tail = remote(tokens.at[0, pl.ds(TOK - CAP, CAP)], xp.at[pl.ds(0, CAP)], halo_s.at[0], halo_r.at[0], b, lax.rem(s + 1, seqs))
    head = remote(tokens.at[0, pl.ds(0, CAP)], xp.at[pl.ds(TOK + CAP, CAP)], halo_s.at[1], halo_r.at[1], b, lax.rem(s + seqs - 1, seqs))
    tail.start()
    head.start()
    send(1, 0)
    send(1, 1)
    locals_ = [
        pltpu.make_async_copy(args[a], views[a](OWN), local_sem.at[a]) for a in range(3)
    ]
    for cp in locals_:
        cp.start()

    xp[pl.ds(CAP, TOK)] = tokens[0]
    xp[pl.ds(TOK + 2 * CAP, 32)] = jnp.zeros((32, D), BF16)
    row, col = iota((512, HEADS * TAPS), 0), iota((512, HEADS * TAPS), 1)
    tap = row & 31
    spread = ((col == (row >> 5) * TAPS + tap) & (tap < TAPS)).astype(F32).astype(BF16)
    kw = dot(spread, kwt[...]).astype(BF16)
    for q in range(4):
        logits = dot_nt(kw[q * 128 : (q + 1) * 128], tokens[0]).reshape(4, 32, TOK)
        logits = jnp.where(iota(logits.shape, 1) < TAPS, logits, -3e38)
        e = jnp.exp(logits - jnp.max(logits, axis=1, keepdims=True))
        p = e / jnp.sum(e, axis=1, keepdims=True)
        pt[q] = p.astype(BF16).astype(F32).reshape(128, TOK).T

    tail.wait_recv()
    head.wait_recv()
    first, last = (s > 0).astype(F32), (s < seqs - 1).astype(F32)
    xp[pl.ds(0, CAP)] = (xp[pl.ds(0, CAP)].astype(F32) * first).astype(BF16)
    xp[pl.ds(TOK + CAP, CAP)] = (xp[pl.ds(TOK + CAP, CAP)].astype(F32) * last).astype(BF16)

    lane = iota((64, 128), 1)
    for q in range(4):
        for t in range(TOK // 64):
            p = pt[q, pl.ds(t * 64, 64)]
            bands = []
            for i in range(4):
                mine_only = jnp.where((lane >> 5) == i, p, 0.0)
                bands.append(
                    pltpu.roll(mine_only, (1 - 32 * i) % 128, 1, stride=1, stride_axis=0).astype(BF16)
                )
            for i in range(2):
                cols = pl.ds((2 * q + i) * 128, 128)
                window = xp[pl.ds(t * 64, 128), cols]
                conv = jnp.where(lane < 64, dot(bands[2 * i], window), dot(bands[2 * i + 1], window))
                mixed[pl.ds(t * 64, 64), cols] = conv + tokens[0, pl.ds(t * 64, 64), cols].astype(F32)

    m = mixed[...]
    scale = lax.rsqrt(jnp.mean(m * m, axis=1, keepdims=True) + EPS)
    normed[...] = (m * scale * gain[...].astype(F32)).astype(BF16)
    one_c = idc[...] == iota((TOK, EXPERTS), 1)
    one_r = idr[...] == iota((EXPERTS, TOK), 0)
    fc, fr = one_c.astype(F32), one_r.astype(F32)
    up_tri = (iota((TOK, TOK), 0) < iota((TOK, TOK), 1)).astype(F32).astype(BF16)
    lo_tri = (iota((TOK, TOK), 0) > iota((TOK, TOK), 1)).astype(F32).astype(BF16)
    rank_c = jnp.sum(dot(lo_tri, fc.astype(BF16)) * fc, axis=1, keepdims=True)
    rank_r = jnp.sum(dot(fr.astype(BF16), up_tri) * fr, axis=0, keepdims=True)
    cap_c = jnp.sum(fc * capr[...].astype(F32), axis=1, keepdims=True)
    cap_r = jnp.sum(fr * capc[...].astype(F32), axis=0, keepdims=True)
    slot_c = jnp.where(rank_c < cap_c, idc[...].astype(F32) * CAP + rank_c, -1.0)
    slot_r = jnp.where(rank_r < cap_r, idr[...].astype(F32) * CAP + rank_r, -1.0)
    sel[...] = (slot_c == iota((TOK, SLOTS), 1).astype(F32)).astype(F32).astype(BF16)
    sel_t = (slot_r == iota((SLOTS, TOK), 0).astype(F32)).astype(F32).astype(BF16)
    chosen = jnp.sum(dot_nt(normed[...], router[...]) * fc, axis=1, keepdims=True)
    gate_s[...] = 1.0 / (1.0 + jnp.exp(-chosen))
    packed[...] = dot(sel_t, normed[...]).astype(BF16)

    place = (x * NC + c) * CAP

    def aligned(v):
        return pl.multiple_of(v, CAP)

    def home(dh):
        return ((lo, 0), (0, 1 + lo), (1 - lo, 3), (1, 1 + lo))[dh]

    for dh in (2, 1, 3, 0):
        home_lo, kind = home(dh)
        to_h = lax.rem(h + dh, NH)

        def to(i, _, home_lo=home_lo, kind=kind, to_h=to_h):
            tx, tc = lax.rem(x + i // NC, NX), lax.rem(c + lax.rem(i, NC), NC)
            e = (tx * NH + to_h) * NC + tc
            remote(
                packed.at[pl.ds(aligned(e * CAP), CAP)],
                rows.at[pl.ds(aligned(kind * GROUP + place), CAP)],
                fwd_s, fwd_r.at[kind], home_lo * NY + y, e,
            ).start()
            return 0

        lax.fori_loop(1 if dh == 0 else 0, NX * NC, to, 0)
    rows[pl.ds(aligned(place), CAP)] = packed[pl.ds(aligned(s * CAP), CAP)]

    send(1, 2)
    forward(1, 0)
    forward(1, 1)

    ex = []

    def exchange(kind):
        n = GROUP - CAP if kind == 0 else GROUP
        block = rows.at[pl.ds(0, n)]
        remote(block, block, fwd_s, fwd_r.at[kind], b, s).wait_recv()
        src = rows.at[pl.ds(kind * GROUP, GROUP)]
        dst = rows.at[pl.ds(SLOTS + kind * GROUP, GROUP)]
        cp = remote(src, dst, ex_s.at[kind], ex_r.at[kind], pair, s)
        cp.start()
        ex.append(cp)

    exchange(0)
    forward(1, 2)
    forward(2, 0)
    forward(2, 1)
    exchange(1)
    exchange(2)
    exchange(3)
    forward(2, 2)
    for cp in locals_:
        cp.wait()

    def units(slot):
        def body(i, _):
            r = pl.ds(pl.multiple_of(i * 256, 256), 256)
            v = dot(rows[r], gu[slot])
            g, u = v[:, :PIECE], v[:, PIECE:]
            act[r, pl.ds(slot * PIECE, PIECE)] = (g / (1.0 + jnp.exp(-g)) * u).astype(BF16)
            return 0

        lax.fori_loop(0, 2 * SLOTS // 256, body, 0)

    for cp in ex:
        cp.wait_recv()
    units(0)
    forward(3, 0)
    forward(3, 1)
    for slot in (1, 4, 2, 5, 3, 6):
        units(slot)
    forward(3, 2)
    hop(0, 4, 0).wait_recv()
    hop(1, 4, 1).wait_recv()
    units(7)
    hop(0, 4, 2).wait_recv()
    hop(1, 4, 2).wait_recv()

    px = []
    for j in range(PARTS):
        def down(i, _, j=j):
            r = pl.ds(pl.multiple_of(i * 256, 256), 256)
            r2 = pl.ds(pl.multiple_of(SLOTS + i * 256, 256), 256)
            ps[j, r] = dot_nt(act[r2], wd[pl.ds(j * FEAT, FEAT)]).astype(BF16)
            return 0

        lax.fori_loop(0, SLOTS // 256, down, 0)
        cp = remote(ps.at[j], pr.at[j], px_s.at[j], px_r.at[j], pair, s)
        cp.start()
        px.append(cp)

    for j in range(PARTS):
        def down_own(i, _, j=j):
            r = pl.ds(pl.multiple_of(i * 256, 256), 256)
            mine[j, r] = dot_nt(act[r], wd[pl.ds(j * FEAT, FEAT)])
            return 0

        lax.fori_loop(0, SLOTS // 256, down_own, 0)

    for j in range(PARTS):
        px[j].wait_recv()
        bs[j] = (mine[j] + pr[j].astype(F32)).astype(BF16)
        near = lax.rem(h + NH - 1 + 2 * lo, NH)
        for kind in (3, 1, 2, 0):
            to_h = (h, near, near, lax.rem(h + 2, NH))[kind]
            to_lo = (lo, 0, 1, 1 - lo)[kind]

            def back(i, _, kind=kind, to_h=to_h, to_lo=to_lo, j=j):
                tx, tc = lax.rem(x + i // NC, NX), lax.rem(c + lax.rem(i, NC), NC)
                t = (tx * NH + to_h) * NC + tc
                remote(
                    bs.at[j, pl.ds(aligned(kind * GROUP + (tx * NC + tc) * CAP), CAP)],
                    bk.at[j, pl.ds(aligned(s * CAP), CAP)],
                    ret_s.at[j], ret_r.at[j], to_lo * NY + y, t,
                ).start()
                return 0

            lax.fori_loop(1 if kind == 0 else 0, NX * NC, back, 0)
        bk[j, pl.ds(aligned(s * CAP), CAP)] = bs[j, pl.ds(aligned(place), CAP)]

    for j in range(PARTS):
        block = bk.at[j, pl.ds(0, SLOTS - CAP)]
        remote(block, block, ret_s.at[j], ret_r.at[j], b, s).wait_recv()
        cols = pl.ds(j * FEAT, FEAT)
        out[0, :, cols] = (mixed[:, cols] + gate_s[...] * dot(sel[...], bk[j])).astype(BF16)

    tail.wait_send()
    head.wait_send()
    for cp in hops + ex + px:
        cp.wait_send()
    block = packed.at[pl.ds(0, SLOTS - CAP)]
    remote(block, block, fwd_s, fwd_r.at[0], b, s).wait_send()
    for j in range(PARTS):
        block = bs.at[j, pl.ds(0, SLOTS - CAP)]
        remote(block, block, ret_s.at[j], ret_r.at[j], b, s).wait_send()


def on_device(tokens, expert_ids, expert_capacity, kernel_weight, norm_gain, router, expert_gate, expert_up, expert_down):
    dma = pltpu.SemaphoreType.DMA
    vmem = pl.BlockSpec(memory_space=pltpu.VMEM)
    anywhere = pl.BlockSpec(memory_space=pl.ANY)
    return pl.pallas_call(
        layer,
        out_shape=jax.ShapeDtypeStruct((1, TOK, D), BF16),
        in_specs=[vmem] * 8 + [anywhere] * 3,
        out_specs=vmem,
        scratch_shapes=[
            pltpu.VMEM((TOK + 4 * CAP, D), BF16),
            pltpu.VMEM((4, TOK, 128), F32),
            pltpu.VMEM((TOK, D), F32),
            pltpu.VMEM((TOK, D), BF16),
            pltpu.VMEM((SLOTS, D), BF16),
            pltpu.VMEM((TOK, SLOTS), BF16),
            pltpu.VMEM((TOK, 1), F32),
            pltpu.VMEM((2 * SLOTS, D), BF16),
            pltpu.VMEM((NY, D, 2 * PIECE), BF16),
            pltpu.VMEM((D, NY * PIECE), BF16),
            pltpu.VMEM((2 * SLOTS, NY * PIECE), BF16),
            pltpu.VMEM((PARTS, SLOTS, FEAT), BF16),
            pltpu.VMEM((PARTS, SLOTS, FEAT), BF16),
            pltpu.VMEM((PARTS, SLOTS, FEAT), F32),
            pltpu.VMEM((PARTS, SLOTS, FEAT), BF16),
            pltpu.VMEM((PARTS, SLOTS, FEAT), BF16),
            dma((3,)),
            dma((2,)), dma((2,)),
            dma((2, 4, 3)), dma((2, 4, 3)),
            dma, dma((4,)),
            dma((4,)), dma((4,)),
            dma((PARTS,)), dma((PARTS,)),
            dma((PARTS,)), dma((PARTS,)),
        ],
        compiler_params=pltpu.CompilerParams(
            collective_id=0, has_side_effects=True, vmem_limit_bytes=56 * 1024 * 1024
        ),
    )(
        tokens,
        expert_ids.reshape(TOK, 1),
        expert_ids.reshape(1, TOK),
        expert_capacity.reshape(EXPERTS, 1),
        expert_capacity.reshape(1, EXPERTS),
        kernel_weight.T,
        norm_gain.reshape(1, D),
        router.T,
        expert_gate,
        expert_up,
        expert_down,
    )


def solution(mesh):
    placed = (
        P("blk", "seq", None),
        P("blk", "seq", None),
        P(),
        P(),
        P(),
        P(),
        P("seq", None, "blk"),
        P("seq", None, "blk"),
        P("seq", None, "blk"),
    )
    return jax.shard_map(
        on_device, mesh=mesh, in_specs=placed, out_specs=P("blk", "seq", None), check_vma=False
    )
```

```python
import functools

import jax
import jax.numpy as jnp
from jax import lax
from jax.experimental import pallas as pl
from jax.experimental.pallas import tpu as pltpu
from jax.sharding import PartitionSpec as P

MESH = pl.DeviceIdType.MESH
F32 = jnp.float32
BF16 = jnp.bfloat16

D = 1024
HEADS = 16
TAPS = 31
HALF = 15
TOK = 256
EXPERTS = 32
CAP = 16
SLOTS = EXPERTS * CAP
EPS = 1e-06

NX, NH, NC, NY = 4, 4, 2, 8
GROUP = NX * NC * CAP
PIECE = 128
PARTS = 4
FEAT = D // PARTS
BLOCKS = 4
BLOCK = D // BLOCKS
HALF_ROWS = SLOTS // 2
AHEAD = 2

OWN, FAR = 0, 7
LEFT = (0, 1, 2, 3, 7)
RIGHT = (0, 4, 5, 6, 7)


def dot(a, b):
    return jnp.dot(a, b, preferred_element_type=F32)


def dot_nt(a, b):
    return lax.dot_general(a, b, (((1,), (1,)), ((), ())), preferred_element_type=F32)


def iota(shape, dim):
    return lax.broadcasted_iota(jnp.int32, shape, dim)


def layer(
    tokens, ids, limits, kwt, gain, router, gate_w, up_w, down_w,
    out,
    xp, pt, mixed, normed, packed, sel, gate_s,
    rows, gu, wd, act, ps, pr, mine, bs, bk,
    local_sem, halo_s, halo_r, ag_s, ag_r, fwd_s, fwd_r, ex_s, ex_r, px_s, px_r, ret_s, ret_r,
):
    s = lax.axis_index("seq")
    b = lax.axis_index("blk")
    lo, y = b // NY, lax.rem(b, NY)
    c = lax.rem(s, NC)
    h = lax.rem(s // NC, NH)
    x = s // (NC * NH)
    right = lo * NY + lax.rem(y + 1, NY)
    left = lo * NY + lax.rem(y + NY - 1, NY)
    pair = (1 - lo) * NY + y
    seqs = NX * NH * NC

    barrier = pltpu.get_barrier_semaphore()

    for dh, to_lo in ((0, lo), (1, lo), (3, lo), (3 - 2 * lo, 1 - lo), (2, 1 - lo)):
        def greet(i, _, dh=dh, to_lo=to_lo):
            t = (lax.rem(x + i // NC, NX) * NH + lax.rem(h + dh, NH)) * NC + lax.rem(c + lax.rem(i, NC), NC)
            pl.semaphore_signal(barrier, inc=1, device_id=(to_lo * NY + y, t), device_id_type=MESH)
            return 0

        lax.fori_loop(1 if isinstance(dh, int) and dh == 0 else 0, NX * NC, greet, 0)
    for t in (pair, left, right):
        pl.semaphore_signal(barrier, inc=1, device_id=(t, s), device_id_type=MESH)
    pl.semaphore_wait(barrier, 5 * NX * NC - 1 + 3)

    def remote(src, dst, ss, rs, blk, seq):
        return pltpu.make_async_remote_copy(
            src_ref=src, dst_ref=dst, send_sem=ss, recv_sem=rs, device_id=(blk, seq), device_id_type=MESH
        )

    def g_view(slot):
        return gu.at[slot, :, pl.ds(0, PIECE)]

    def u_view(slot):
        return gu.at[slot, :, pl.ds(PIECE, PIECE)]

    def d_view(slot, start, size):
        return wd.at[pl.ds(start, size), pl.ds(slot * PIECE, PIECE)]

    def view(a, slot):
        return (g_view, u_view)[a](slot) if a < 2 else d_view(slot, (a - 2) * BLOCK, BLOCK)

    def owned(a):
        return (gate_w, up_w)[a].at[0] if a < 2 else down_w.at[0, pl.ds((a - 2) * BLOCK, BLOCK)]

    def hop(way, step, a):
        slots = (LEFT, RIGHT)[way]
        if step == 4 and a >= 2:
            start = (a - 2) * BLOCK + way * BLOCK // 2
            src, dst = d_view(slots[3], start, BLOCK // 2), d_view(FAR, start, BLOCK // 2)
        else:
            src = owned(a) if step == 1 else view(a, slots[step - 1])
            dst = view(a, slots[step])
        return remote(src, dst, ag_s.at[way, step - 1, a], ag_r.at[way, step - 1, a], (right, left)[way], s)

    hops = []

    def send(step, a):
        for way in range(2):
            cp = hop(way, step, a)
            cp.start()
            hops.append(cp)

    def forward(step, a):
        for way in range(2):
            hop(way, step, a).wait_recv()
            if step < 3 or a >= 2 or a == way:
                cp = hop(way, step + 1, a)
                cp.start()
                hops.append(cp)

    tail = remote(tokens.at[0, pl.ds(TOK - CAP, CAP)], xp.at[pl.ds(0, CAP)], halo_s.at[0], halo_r.at[0], b, lax.rem(s + 1, seqs))
    head = remote(tokens.at[0, pl.ds(0, CAP)], xp.at[pl.ds(TOK + CAP, CAP)], halo_s.at[1], halo_r.at[1], b, lax.rem(s + seqs - 1, seqs))
    tail.start()
    head.start()
    send(1, 0)
    send(1, 1)
    locals_ = [
        pltpu.make_async_copy(owned(a), view(a, OWN), local_sem.at[a]) for a in range(2 + BLOCKS)
    ]
    for cp in locals_:
        cp.start()

    xp[pl.ds(CAP, TOK)] = tokens[0]
    xp[pl.ds(TOK + 2 * CAP, 32)] = jnp.zeros((32, D), BF16)
    row, col = iota((512, HEADS * TAPS), 0), iota((512, HEADS * TAPS), 1)
    tap = row & 31
    spread = ((col == (row >> 5) * TAPS + tap) & (tap < TAPS)).astype(F32).astype(BF16)
    kw = dot(spread, kwt[...]).astype(BF16)
    for q in range(4):
        logits = dot_nt(kw[q * 128 : (q + 1) * 128], tokens[0]).reshape(4, 32, TOK)
        logits = jnp.where(iota(logits.shape, 1) < TAPS, logits, -3e38)
        e = jnp.exp(logits - jnp.max(logits, axis=1, keepdims=True))
        p = e / jnp.sum(e, axis=1, keepdims=True)
        pt[q] = p.astype(BF16).astype(F32).reshape(128, TOK).T

    tail.wait_recv()
    head.wait_recv()
    first, last = (s > 0).astype(F32), (s < seqs - 1).astype(F32)
    xp[pl.ds(0, CAP)] = (xp[pl.ds(0, CAP)].astype(F32) * first).astype(BF16)
    xp[pl.ds(TOK + CAP, CAP)] = (xp[pl.ds(TOK + CAP, CAP)].astype(F32) * last).astype(BF16)

    lane = iota((64, 128), 1)
    for q in range(4):
        for t in range(TOK // 64):
            p = pt[q, pl.ds(t * 64, 64)]
            bands = []
            for i in range(4):
                mine_only = jnp.where((lane >> 5) == i, p, 0.0)
                bands.append(
                    pltpu.roll(mine_only, (1 - 32 * i) % 128, 1, stride=1, stride_axis=0).astype(BF16)
                )
            for i in range(2):
                cols = pl.ds((2 * q + i) * 128, 128)
                window = xp[pl.ds(t * 64, 128), cols]
                conv = jnp.where(lane < 64, dot(bands[2 * i], window), dot(bands[2 * i + 1], window))
                mixed[pl.ds(t * 64, 64), cols] = conv + tokens[0, pl.ds(t * 64, 64), cols].astype(F32)

    m = mixed[...]
    scale = lax.rsqrt(jnp.mean(m * m, axis=1, keepdims=True) + EPS)
    normed[...] = (m * scale * gain[...].reshape(1, D).astype(F32)).astype(BF16)
    same = (iota((TOK, TOK), 0) == iota((TOK, TOK), 1)).astype(F32)
    idr = ids[...].astype(F32)
    idc = jnp.sum(same * idr, axis=1, keepdims=True)
    capr = limits[...].astype(F32)
    capc = jnp.sum(same[:EXPERTS, :EXPERTS] * capr, axis=1, keepdims=True)
    fc = (idc == iota((TOK, EXPERTS), 1).astype(F32)).astype(F32)
    fr = (idr == iota((EXPERTS, TOK), 0).astype(F32)).astype(F32)
    up_tri = (iota((TOK, TOK), 0) < iota((TOK, TOK), 1)).astype(F32).astype(BF16)
    lo_tri = (iota((TOK, TOK), 0) > iota((TOK, TOK), 1)).astype(F32).astype(BF16)
    rank_c = jnp.sum(dot(lo_tri, fc.astype(BF16)) * fc, axis=1, keepdims=True)
    rank_r = jnp.sum(dot(fr.astype(BF16), up_tri) * fr, axis=0, keepdims=True)
    cap_c = jnp.sum(fc * capr, axis=1, keepdims=True)
    cap_r = jnp.sum(fr * capc, axis=0, keepdims=True)
    slot_c = jnp.where(rank_c < cap_c, idc * CAP + rank_c, -1.0)
    slot_r = jnp.where(rank_r < cap_r, idr * CAP + rank_r, -1.0)
    sel[...] = (slot_c == iota((TOK, SLOTS), 1).astype(F32)).astype(F32).astype(BF16)
    sel_t = (slot_r == iota((SLOTS, TOK), 0).astype(F32)).astype(F32).astype(BF16)
    chosen = jnp.sum(dot_nt(normed[...], router[...]) * fc, axis=1, keepdims=True)
    gate_s[...] = 1.0 / (1.0 + jnp.exp(-chosen))
    packed[...] = dot(sel_t, normed[...]).astype(BF16)

    place = (x * NC + c) * CAP

    def aligned(v):
        return pl.multiple_of(v, CAP)

    def home(dh):
        return ((lo, 0), (0, 1 + lo), (1 - lo, 3), (1, 1 + lo))[dh]

    for dh in (0, 1, 3, 2):
        home_lo, kind = home(dh)
        to_h = lax.rem(h + dh, NH)

        def to(i, _, home_lo=home_lo, kind=kind, to_h=to_h):
            tx, tc = lax.rem(x + i // NC, NX), lax.rem(c + lax.rem(i, NC), NC)
            e = (tx * NH + to_h) * NC + tc
            remote(
                packed.at[pl.ds(aligned(e * CAP), CAP)],
                rows.at[pl.ds(aligned(kind * GROUP + place), CAP)],
                fwd_s, fwd_r.at[kind], home_lo * NY + y, e,
            ).start()
            return 0

        lax.fori_loop(1 if dh == 0 else 0, NX * NC, to, 0)
    rows[pl.ds(aligned(place), CAP)] = packed[pl.ds(aligned(s * CAP), CAP)]

    ex = []

    def exchange(kind):
        n = GROUP - CAP if kind == 0 else GROUP
        block = rows.at[pl.ds(0, n)]
        remote(block, block, fwd_s, fwd_r.at[kind], b, s).wait_recv()
        src = rows.at[pl.ds(kind * GROUP, GROUP)]
        dst = rows.at[pl.ds(SLOTS + kind * GROUP, GROUP)]
        cp = remote(src, dst, ex_s.at[kind], ex_r.at[kind], pair, s)
        cp.start()
        ex.append(cp)

    def units(blocks, *slots):
        for slot in slots:
            for k in blocks:
                r = pl.ds(k * HALF_ROWS, HALF_ROWS)
                v = dot(rows[r], gu[slot])
                g, u = v[:, :PIECE], v[:, PIECE:]
                act[r, pl.ds(slot * PIECE, PIECE)] = (g / (1.0 + jnp.exp(-g)) * u).astype(BF16)

    forward(1, 0)
    forward(1, 1)
    exchange(0)
    send(1, 2)
    forward(2, 0)
    forward(2, 1)
    forward(1, 2)
    exchange(1)
    exchange(2)
    exchange(3)
    for cp in locals_:
        cp.wait()
    forward(3, 0)
    forward(3, 1)
    forward(2, 2)
    send(1, 3)
    units((0, 1), 0, 1, 4, 2, 5)
    forward(3, 2)
    forward(1, 3)
    send(1, 4)
    units((0, 1), 3, 6)
    hop(0, 4, 0).wait_recv()
    hop(1, 4, 1).wait_recv()
    forward(2, 3)
    forward(1, 4)
    send(1, 5)
    units((0, 1), 7)
    ex[0].wait_recv()
    ex[1].wait_recv()
    units((2,), 0, 1, 4, 2, 5, 3, 6, 7)
    ex[2].wait_recv()
    ex[3].wait_recv()
    units((3,), 0, 1, 4, 2, 5, 3, 6, 7)

    order = [(j, i) for j in range(PARTS) for i in (1, 0)]

    def down(k, j):
        return dot_nt(act[pl.ds(k * HALF_ROWS, HALF_ROWS)], wd[pl.ds(j * FEAT, FEAT)])

    def part_of(ref, j, i):
        return ref.at[j, pl.ds(i * HALF_ROWS, HALF_ROWS)]

    px = [
        remote(part_of(ps, j, i), part_of(pr, j, i), px_s.at[n], px_r.at[n], pair, s)
        for n, (j, i) in enumerate(order)
    ]
    near = lax.rem(h + NH - 1 + 2 * lo, NH)

    def give(j, i):
        r = pl.ds(i * HALF_ROWS, HALF_ROWS)
        bs[j, r] = (mine[j, r] + pr[j, r].astype(F32)).astype(BF16)
        for kind in ((1, 0), (3, 2))[i]:
            to_h = (h, near, near, lax.rem(h + 2, NH))[kind]
            to_lo = (lo, 0, 1, 1 - lo)[kind]

            def back(n, _, kind=kind, to_h=to_h, to_lo=to_lo):
                tx, tc = lax.rem(x + n // NC, NX), lax.rem(c + lax.rem(n, NC), NC)
                t = (tx * NH + to_h) * NC + tc
                remote(
                    bs.at[j, pl.ds(aligned(kind * GROUP + (tx * NC + tc) * CAP), CAP)],
                    bk.at[j, pl.ds(aligned(s * CAP), CAP)],
                    ret_s.at[j], ret_r.at[j], to_lo * NY + y, t,
                ).start()
                return 0

            lax.fori_loop(1 if kind == 0 else 0, NX * NC, back, 0)
        if i == 0:
            bk[j, pl.ds(aligned(s * CAP), CAP)] = bs[j, pl.ds(aligned(place), CAP)]

    def arrived(a):
        for way in range(2):
            hop(way, 4, a).wait_recv()

    passing = {0: ((3, 3), (2, 4), (1, 5)), 1: ((3, 4), (2, 5)), 2: ((3, 5),)}
    for n, (j, i) in enumerate(order):
        if n % 2 == 0:
            arrived(2 + j * BLOCKS // PARTS)
        r = pl.ds(i * HALF_ROWS, HALF_ROWS)
        ps[j, r] = down(2 + i, j).astype(BF16)
        if n >= AHEAD:
            px[n - AHEAD].wait_recv()
        px[n].start()
        mine[j, r] = down(i, j)
        if n >= AHEAD:
            give(*order[n - AHEAD])
        for step, a in passing.get(n, ()):
            forward(step, a)
    for n in range(len(order) - AHEAD, len(order)):
        px[n].wait_recv()
        give(*order[n])

    for j in range(PARTS):
        block = bk.at[j, pl.ds(0, SLOTS - CAP)]
        remote(block, block, ret_s.at[j], ret_r.at[j], b, s).wait_recv()
        cols = pl.ds(j * FEAT, FEAT)
        out[0, :, cols] = (mixed[:, cols] + gate_s[...] * dot(sel[...], bk[j])).astype(BF16)

    tail.wait_send()
    head.wait_send()
    for cp in hops + ex + px:
        cp.wait_send()
    block = packed.at[pl.ds(0, SLOTS - CAP)]
    remote(block, block, fwd_s, fwd_r.at[0], b, s).wait_send()
    for j in range(PARTS):
        block = bs.at[j, pl.ds(0, SLOTS - CAP)]
        remote(block, block, ret_s.at[j], ret_r.at[j], b, s).wait_send()


def on_device(tokens, expert_ids, expert_capacity, kernel_weight, norm_gain, router, expert_gate, expert_up, expert_down):
    dma = pltpu.SemaphoreType.DMA
    vmem = pl.BlockSpec(memory_space=pltpu.VMEM)
    anywhere = pl.BlockSpec(memory_space=pl.ANY)
    return pl.pallas_call(
        layer,
        out_shape=jax.ShapeDtypeStruct((1, TOK, D), BF16),
        in_specs=[vmem] * 6 + [anywhere] * 3,
        out_specs=vmem,
        scratch_shapes=[
            pltpu.VMEM((TOK + 4 * CAP, D), BF16),
            pltpu.VMEM((4, TOK, 128), F32),
            pltpu.VMEM((TOK, D), F32),
            pltpu.VMEM((TOK, D), BF16),
            pltpu.VMEM((SLOTS, D), BF16),
            pltpu.VMEM((TOK, SLOTS), BF16),
            pltpu.VMEM((TOK, 1), F32),
            pltpu.VMEM((2 * SLOTS, D), BF16),
            pltpu.VMEM((NY, D, 2 * PIECE), BF16),
            pltpu.VMEM((D, NY * PIECE), BF16),
            pltpu.VMEM((2 * SLOTS, NY * PIECE), BF16),
            pltpu.VMEM((PARTS, SLOTS, FEAT), BF16),
            pltpu.VMEM((PARTS, SLOTS, FEAT), BF16),
            pltpu.VMEM((PARTS, SLOTS, FEAT), F32),
            pltpu.VMEM((PARTS, SLOTS, FEAT), BF16),
            pltpu.VMEM((PARTS, SLOTS, FEAT), BF16),
            dma((2 + BLOCKS,)),
            dma((2,)), dma((2,)),
            dma((2, 4, 2 + BLOCKS)), dma((2, 4, 2 + BLOCKS)),
            dma, dma((4,)),
            dma((4,)), dma((4,)),
            dma((2 * PARTS,)), dma((2 * PARTS,)),
            dma((PARTS,)), dma((PARTS,)),
        ],
        compiler_params=pltpu.CompilerParams(
            collective_id=0, has_side_effects=True, vmem_limit_bytes=56 * 1024 * 1024
        ),
    )(
        tokens,
        expert_ids.reshape(1, TOK),
        expert_capacity.reshape(1, EXPERTS),
        kernel_weight.T,
        norm_gain,
        router.T,
        expert_gate,
        expert_up,
        expert_down,
    )


def solution(mesh):
    placed = (
        P("blk", "seq", None),
        P("blk", "seq", None),
        P(),
        P(),
        P(),
        P(),
        P("seq", None, "blk"),
        P("seq", None, "blk"),
        P("seq", None, "blk"),
    )
    return jax.shard_map(
        on_device, mesh=mesh, in_specs=placed, out_specs=P("blk", "seq", None), check_vma=False
    )
```

```python
import functools

import jax
import jax.numpy as jnp
from jax import lax
from jax.experimental import pallas as pl
from jax.experimental.pallas import tpu as pltpu
from jax.sharding import PartitionSpec as P

MESH = pl.DeviceIdType.MESH
F32 = jnp.float32
BF16 = jnp.bfloat16

D = 1024
HEADS = 16
TAPS = 31
HALF = 15
TOK = 256
EXPERTS = 32
CAP = 16
SLOTS = EXPERTS * CAP
EPS = 1e-06

NX, NH, NC, NY = 4, 4, 2, 8
GROUP = NH * NC * CAP
PIECE = 128
PARTS = 4
FEAT = D // PARTS
BLOCKS = 4
BLOCK = D // BLOCKS
HALF_ROWS = SLOTS // 2
AHEAD = 2

OWN, FAR = 0, 7
LEFT = (0, 1, 2, 3, 7)
RIGHT = (0, 4, 5, 6, 7)


def dot(a, b):
    return jnp.dot(a, b, preferred_element_type=F32)


def dot_nt(a, b):
    return lax.dot_general(a, b, (((1,), (1,)), ((), ())), preferred_element_type=F32)


def iota(shape, dim):
    return lax.broadcasted_iota(jnp.int32, shape, dim)


def layer(
    tokens, ids, limits, kwt, gain, router, gate_w, up_w, down_w,
    out,
    xp, kw_in, pt, mixed, normed, packed, sel, gate_s,
    rows, gu, wd, act, ps, pr, mine, bs, bk,
    in_sem, local_sem, halo_s, halo_r, ag_s, ag_r, fwd_s, fwd_r, ex_s, ex_r, px_s, px_r, ret_s, ret_r,
):
    s = lax.axis_index("seq")
    b = lax.axis_index("blk")
    lo, y = b // NY, lax.rem(b, NY)
    c = lax.rem(s, NC)
    h = lax.rem(s // NC, NH)
    x = s // (NC * NH)
    right = lo * NY + lax.rem(y + 1, NY)
    left = lo * NY + lax.rem(y + NY - 1, NY)
    pair = (1 - lo) * NY + y
    seqs = NX * NH * NC

    here = pl.ds(CAP, TOK)
    inputs = [
        pltpu.make_async_copy(tokens.at[0], xp.at[here], in_sem.at[0]),
        pltpu.make_async_copy(kwt, kw_in, in_sem.at[1]),
    ]
    for cp in inputs:
        cp.start()

    barrier = pltpu.get_barrier_semaphore()

    for dh, to_lo in ((0, lo), (1, lo), (3, lo), (3 - 2 * lo, 1 - lo), (2, 1 - lo)):
        def greet(i, _, dh=dh, to_lo=to_lo):
            t = (lax.rem(x + i // NC, NX) * NH + lax.rem(h + dh, NH)) * NC + lax.rem(c + lax.rem(i, NC), NC)
            pl.semaphore_signal(barrier, inc=1, device_id=(to_lo * NY + y, t), device_id_type=MESH)
            return 0

        lax.fori_loop(1 if isinstance(dh, int) and dh == 0 else 0, NX * NC, greet, 0)
    for t in (pair, left, right):
        pl.semaphore_signal(barrier, inc=1, device_id=(t, s), device_id_type=MESH)
    pl.semaphore_wait(barrier, 5 * NX * NC - 1 + 3)

    def remote(src, dst, ss, rs, blk, seq):
        return pltpu.make_async_remote_copy(
            src_ref=src, dst_ref=dst, send_sem=ss, recv_sem=rs, device_id=(blk, seq), device_id_type=MESH
        )

    def g_view(slot):
        return gu.at[slot, :, pl.ds(0, PIECE)]

    def u_view(slot):
        return gu.at[slot, :, pl.ds(PIECE, PIECE)]

    def d_view(slot, start, size):
        return wd.at[pl.ds(start, size), pl.ds(slot * PIECE, PIECE)]

    def view(a, slot):
        return (g_view, u_view)[a](slot) if a < 2 else d_view(slot, (a - 2) * BLOCK, BLOCK)

    def owned(a):
        return (gate_w, up_w)[a].at[0] if a < 2 else down_w.at[0, pl.ds((a - 2) * BLOCK, BLOCK)]

    def hop(way, step, a):
        slots = (LEFT, RIGHT)[way]
        if step == 4 and a >= 2:
            start = (a - 2) * BLOCK + way * BLOCK // 2
            src, dst = d_view(slots[3], start, BLOCK // 2), d_view(FAR, start, BLOCK // 2)
        else:
            src = owned(a) if step == 1 else view(a, slots[step - 1])
            dst = view(a, slots[step])
        return remote(src, dst, ag_s.at[way, step - 1, a], ag_r.at[way, step - 1, a], (right, left)[way], s)

    hops = []

    def send(step, a):
        for way in range(2):
            cp = hop(way, step, a)
            cp.start()
            hops.append(cp)

    def forward(step, a):
        for way in range(2):
            hop(way, step, a).wait_recv()
            if step < 3 or a >= 2 or a == way:
                cp = hop(way, step + 1, a)
                cp.start()
                hops.append(cp)

    tail = remote(tokens.at[0, pl.ds(TOK - CAP, CAP)], xp.at[pl.ds(0, CAP)], halo_s.at[0], halo_r.at[0], b, lax.rem(s + 1, seqs))
    head = remote(tokens.at[0, pl.ds(0, CAP)], xp.at[pl.ds(TOK + CAP, CAP)], halo_s.at[1], halo_r.at[1], b, lax.rem(s + seqs - 1, seqs))
    tail.start()
    head.start()
    send(1, 0)
    send(1, 1)
    locals_ = [
        pltpu.make_async_copy(owned(a), view(a, OWN), local_sem.at[a]) for a in range(2 + BLOCKS)
    ]
    for cp in locals_:
        cp.start()

    xp[pl.ds(TOK + 2 * CAP, 32)] = jnp.zeros((32, D), BF16)
    row, col = iota((512, HEADS * TAPS), 0), iota((512, HEADS * TAPS), 1)
    tap = row & 31
    spread = ((col == (row >> 5) * TAPS + tap) & (tap < TAPS)).astype(F32).astype(BF16)
    for cp in inputs:
        cp.wait()
    kw = dot(spread, kw_in[...]).astype(BF16)
    for q in range(4):
        logits = dot_nt(kw[q * 128 : (q + 1) * 128], xp[here]).reshape(4, 32, TOK)
        logits = jnp.where(iota(logits.shape, 1) < TAPS, logits, -3e38)
        e = jnp.exp(logits - jnp.max(logits, axis=1, keepdims=True))
        p = e / jnp.sum(e, axis=1, keepdims=True)
        pt[q] = p.astype(BF16).astype(F32).reshape(128, TOK).T

    tail.wait_recv()
    head.wait_recv()
    first, last = (s > 0).astype(F32), (s < seqs - 1).astype(F32)
    xp[pl.ds(0, CAP)] = (xp[pl.ds(0, CAP)].astype(F32) * first).astype(BF16)
    xp[pl.ds(TOK + CAP, CAP)] = (xp[pl.ds(TOK + CAP, CAP)].astype(F32) * last).astype(BF16)

    lane = iota((64, 128), 1)
    for q in range(4):
        for t in range(TOK // 64):
            p = pt[q, pl.ds(t * 64, 64)]
            bands = []
            for i in range(4):
                mine_only = jnp.where((lane >> 5) == i, p, 0.0)
                bands.append(
                    pltpu.roll(mine_only, (1 - 32 * i) % 128, 1, stride=1, stride_axis=0).astype(BF16)
                )
            for i in range(2):
                cols = pl.ds((2 * q + i) * 128, 128)
                window = xp[pl.ds(t * 64, 128), cols]
                conv = jnp.where(lane < 64, dot(bands[2 * i], window), dot(bands[2 * i + 1], window))
                mixed[pl.ds(t * 64, 64), cols] = conv + xp[pl.ds(CAP + t * 64, 64), cols].astype(F32)

    m = mixed[...]
    scale = lax.rsqrt(jnp.mean(m * m, axis=1, keepdims=True) + EPS)
    normed[...] = (m * scale * gain[...].reshape(1, D).astype(F32)).astype(BF16)
    same = (iota((TOK, TOK), 0) == iota((TOK, TOK), 1)).astype(F32)
    idr = ids[...].astype(F32)
    idc = jnp.sum(same * idr, axis=1, keepdims=True)
    capr = limits[...].astype(F32)
    capc = jnp.sum(same[:EXPERTS, :EXPERTS] * capr, axis=1, keepdims=True)
    fc = (idc == iota((TOK, EXPERTS), 1).astype(F32)).astype(F32)
    fr = (idr == iota((EXPERTS, TOK), 0).astype(F32)).astype(F32)
    up_tri = (iota((TOK, TOK), 0) < iota((TOK, TOK), 1)).astype(F32).astype(BF16)
    lo_tri = (iota((TOK, TOK), 0) > iota((TOK, TOK), 1)).astype(F32).astype(BF16)
    rank_c = jnp.sum(dot(lo_tri, fc.astype(BF16)) * fc, axis=1, keepdims=True)
    rank_r = jnp.sum(dot(fr.astype(BF16), up_tri) * fr, axis=0, keepdims=True)
    cap_c = jnp.sum(fc * capr, axis=1, keepdims=True)
    cap_r = jnp.sum(fr * capc, axis=0, keepdims=True)
    slot_c = jnp.where(rank_c < cap_c, idc * CAP + rank_c, -1.0)
    slot_r = jnp.where(rank_r < cap_r, idr * CAP + rank_r, -1.0)
    sel[...] = (slot_c == iota((TOK, SLOTS), 1).astype(F32)).astype(F32).astype(BF16)
    sel_t = (slot_r == iota((SLOTS, TOK), 0).astype(F32)).astype(F32).astype(BF16)
    chosen = jnp.sum(dot_nt(normed[...], router[...]) * fc, axis=1, keepdims=True)
    gate_s[...] = 1.0 / (1.0 + jnp.exp(-chosen))
    packed[...] = dot(sel_t, normed[...]).astype(BF16)

    def aligned(v):
        return pl.multiple_of(v, CAP)

    def place(dx, kind, core):
        return aligned(dx * GROUP + (kind * NC + core) * CAP)

    def home(dh):
        return ((lo, 0), (0, 1 + lo), (1 - lo, 3), (1, 1 + lo))[dh]

    for dx in range(NX):
        def to(n, _, dx=dx, turns=(2, 1, 3, 0)):
            for dh in turns:
                home_lo, kind = home(dh)
                e = (lax.rem(x + dx, NX) * NH + lax.rem(h + dh, NH)) * NC + lax.rem(c + n, NC)
                remote(
                    packed.at[pl.ds(aligned(e * CAP), CAP)],
                    rows.at[pl.ds(place(dx, kind, c), CAP)],
                    fwd_s, fwd_r.at[dx], home_lo * NY + y, e,
                ).start()
            return 0

        if dx == 0:
            to(0, 0, turns=(2, 1, 3))
        lax.fori_loop(1 if dx == 0 else 0, NC, to, 0)
    rows[pl.ds(place(0, 0, c), CAP)] = packed[pl.ds(aligned(s * CAP), CAP)]

    ex = []

    def exchange(kind):
        n = GROUP - CAP if kind == 0 else GROUP
        block = rows.at[pl.ds(0, n)]
        remote(block, block, fwd_s, fwd_r.at[kind], b, s).wait_recv()
        src = rows.at[pl.ds(kind * GROUP, GROUP)]
        dst = rows.at[pl.ds(SLOTS + kind * GROUP, GROUP)]
        cp = remote(src, dst, ex_s.at[kind], ex_r.at[kind], pair, s)
        cp.start()
        ex.append(cp)

    def units(blocks, *slots):
        for slot in slots:
            for k in blocks:
                r = pl.ds(k * HALF_ROWS, HALF_ROWS)
                v = dot(rows[r], gu[slot])
                g, u = v[:, :PIECE], v[:, PIECE:]
                act[r, pl.ds(slot * PIECE, PIECE)] = (g / (1.0 + jnp.exp(-g)) * u).astype(BF16)

    forward(1, 0)
    forward(1, 1)
    send(1, 2)
    exchange(0)
    for cp in locals_:
        cp.wait()
    forward(2, 0)
    forward(2, 1)
    forward(1, 2)
    exchange(1)
    units((0,), 0, 1, 4, 2, 5)
    exchange(2)
    exchange(3)
    forward(3, 0)
    forward(3, 1)
    forward(2, 2)
    units((1,), 0, 1, 4, 2, 5)
    units((0, 1), 3, 6)
    forward(3, 2)
    send(1, 3)
    ex[0].wait_recv()
    ex[1].wait_recv()
    units((2,), 0, 1, 4, 2, 5, 3, 6)
    send(1, 4)
    ex[2].wait_recv()
    ex[3].wait_recv()
    units((3,), 0, 1, 4, 2, 5, 3, 6)
    hop(0, 4, 0).wait_recv()
    hop(1, 4, 1).wait_recv()
    forward(1, 3)
    send(1, 5)
    units((3, 1, 2, 0), 7)

    order = [(j, i) for j in range(PARTS) for i in (1, 0)]

    def down(k, j):
        return dot_nt(act[pl.ds(k * HALF_ROWS, HALF_ROWS)], wd[pl.ds(j * FEAT, FEAT)])

    def part_of(ref, j, i):
        return ref.at[j, pl.ds(i * HALF_ROWS, HALF_ROWS)]

    px = [
        remote(part_of(ps, j, i), part_of(pr, j, i), px_s.at[n], px_r.at[n], pair, s)
        for n, (j, i) in enumerate(order)
    ]
    near = lax.rem(h + NH - 1 + 2 * lo, NH)

    def give(j, i):
        r = pl.ds(i * HALF_ROWS, HALF_ROWS)
        bs[j, r] = (mine[j, r] + pr[j, r].astype(F32)).astype(BF16)

        def back(n, _, kinds=(3, 1, 2, 0)):
            dx, tc = 2 * i + n // NC, lax.rem(c + lax.rem(n, NC), NC)
            for kind in kinds:
                to_h = (h, near, near, lax.rem(h + 2, NH))[kind]
                to_lo = (lo, 0, 1, 1 - lo)[kind]
                t = (lax.rem(x + NX - dx, NX) * NH + to_h) * NC + tc
                remote(
                    bs.at[j, pl.ds(place(dx, kind, tc), CAP)],
                    bk.at[j, pl.ds(aligned(s * CAP), CAP)],
                    ret_s.at[j], ret_r.at[j], to_lo * NY + y, t,
                ).start()
            return 0

        if i == 0:
            back(0, 0, kinds=(3, 1, 2))
            bk[j, pl.ds(aligned(s * CAP), CAP)] = bs[j, pl.ds(place(0, 0, c), CAP)]
        lax.fori_loop(1 if i == 0 else 0, 2 * NC, back, 0)

    def arrived(a):
        for way in range(2):
            hop(way, 4, a).wait_recv()

    passing = {0: ((2, 3), (1, 4)), 1: ((3, 3), (2, 4), (1, 5)), 2: ((3, 4), (2, 5)), 3: ((3, 5),)}
    for n, (j, i) in enumerate(order):
        if n % 2 == 0:
            arrived(2 + j * BLOCKS // PARTS)
        r = pl.ds(i * HALF_ROWS, HALF_ROWS)
        ps[j, r] = down(2 + i, j).astype(BF16)
        if n >= AHEAD:
            px[n - AHEAD].wait_recv()
        px[n].start()
        mine[j, r] = down(i, j)
        if n >= AHEAD:
            give(*order[n - AHEAD])
        for step, a in passing.get(n, ()):
            forward(step, a)
    for n in range(len(order) - AHEAD, len(order)):
        px[n].wait_recv()
        give(*order[n])

    for j in range(PARTS):
        block = bk.at[j, pl.ds(0, SLOTS - CAP)]
        remote(block, block, ret_s.at[j], ret_r.at[j], b, s).wait_recv()
        cols = pl.ds(j * FEAT, FEAT)
        out[0, :, cols] = (mixed[:, cols] + gate_s[...] * dot(sel[...], bk[j])).astype(BF16)

    tail.wait_send()
    head.wait_send()
    for cp in hops + ex + px:
        cp.wait_send()
    block = packed.at[pl.ds(0, SLOTS - CAP)]
    remote(block, block, fwd_s, fwd_r.at[0], b, s).wait_send()
    for j in range(PARTS):
        block = bs.at[j, pl.ds(0, SLOTS - CAP)]
        remote(block, block, ret_s.at[j], ret_r.at[j], b, s).wait_send()


def on_device(tokens, expert_ids, expert_capacity, kernel_weight, norm_gain, router, expert_gate, expert_up, expert_down):
    dma = pltpu.SemaphoreType.DMA
    vmem = pl.BlockSpec(memory_space=pltpu.VMEM)
    anywhere = pl.BlockSpec(memory_space=pl.ANY)
    return pl.pallas_call(
        layer,
        out_shape=jax.ShapeDtypeStruct((1, TOK, D), BF16),
        in_specs=[anywhere, vmem, vmem, anywhere, vmem, vmem] + [anywhere] * 3,
        out_specs=vmem,
        scratch_shapes=[
            pltpu.VMEM((TOK + 4 * CAP, D), BF16),
            pltpu.VMEM((HEADS * TAPS, D), BF16),
            pltpu.VMEM((4, TOK, 128), F32),
            pltpu.VMEM((TOK, D), F32),
            pltpu.VMEM((TOK, D), BF16),
            pltpu.VMEM((SLOTS, D), BF16),
            pltpu.VMEM((TOK, SLOTS), BF16),
            pltpu.VMEM((TOK, 1), F32),
            pltpu.VMEM((2 * SLOTS, D), BF16),
            pltpu.VMEM((NY, D, 2 * PIECE), BF16),
            pltpu.VMEM((D, NY * PIECE), BF16),
            pltpu.VMEM((2 * SLOTS, NY * PIECE), BF16),
            pltpu.VMEM((PARTS, SLOTS, FEAT), BF16),
            pltpu.VMEM((PARTS, SLOTS, FEAT), BF16),
            pltpu.VMEM((PARTS, SLOTS, FEAT), F32),
            pltpu.VMEM((PARTS, SLOTS, FEAT), BF16),
            pltpu.VMEM((PARTS, SLOTS, FEAT), BF16),
            dma((2,)),
            dma((2 + BLOCKS,)),
            dma((2,)), dma((2,)),
            dma((2, 4, 2 + BLOCKS)), dma((2, 4, 2 + BLOCKS)),
            dma, dma((4,)),
            dma((4,)), dma((4,)),
            dma((2 * PARTS,)), dma((2 * PARTS,)),
            dma((PARTS,)), dma((PARTS,)),
        ],
        compiler_params=pltpu.CompilerParams(
            collective_id=0, has_side_effects=True, vmem_limit_bytes=56 * 1024 * 1024
        ),
    )(
        tokens,
        expert_ids.reshape(1, TOK),
        expert_capacity.reshape(1, EXPERTS),
        kernel_weight.T,
        norm_gain,
        router.T,
        expert_gate,
        expert_up,
        expert_down,
    )


def solution(mesh):
    placed = (
        P("blk", "seq", None),
        P("blk", "seq", None),
        P(),
        P(),
        P(),
        P(),
        P("seq", None, "blk"),
        P("seq", None, "blk"),
        P("seq", None, "blk"),
    )
    return jax.shard_map(
        on_device, mesh=mesh, in_specs=placed, out_specs=P("blk", "seq", None), check_vma=False
    )
```

```python
import functools

import jax
import jax.numpy as jnp
from jax import lax
from jax.experimental import pallas as pl
from jax.experimental.pallas import tpu as pltpu
from jax.sharding import PartitionSpec as P

MESH = pl.DeviceIdType.MESH
F32 = jnp.float32
BF16 = jnp.bfloat16

D = 1024
HEADS = 16
TAPS = 31
HALF = 15
TOK = 256
EXPERTS = 32
CAP = 16
SLOTS = EXPERTS * CAP
EPS = 1e-06

NX, NH, NC, NY = 4, 4, 2, 8
GROUP = NH * NC * CAP
PIECE = 128
PARTS = 4
FEAT = D // PARTS
BLOCKS = 4
BLOCK = D // BLOCKS
HALF_ROWS = SLOTS // 2
AHEAD = 2

OWN, FAR = 0, 7
LEFT = (0, 1, 2, 3, 7)
RIGHT = (0, 4, 5, 6, 7)


def dot(a, b):
    return jnp.dot(a, b, preferred_element_type=F32)


def dot_nt(a, b):
    return lax.dot_general(a, b, (((1,), (1,)), ((), ())), preferred_element_type=F32)


def iota(shape, dim):
    return lax.broadcasted_iota(jnp.int32, shape, dim)


def layer(
    tokens, ids, limits, kwt, gain, router, gate_w, up_w, down_w,
    out,
    xp, kw_in, pt, mixed, normed, packed, sel, gate_s,
    rows, gu, wd, act, ps, pr, mine, bs, bk,
    in_sem, local_sem, halo_s, halo_r, ag_s, ag_r, fwd_s, fwd_r, ex_s, ex_r, px_s, px_r, ret_s, ret_r,
):
    s = lax.axis_index("seq")
    b = lax.axis_index("blk")
    lo, y = b // NY, lax.rem(b, NY)
    c = lax.rem(s, NC)
    h = lax.rem(s // NC, NH)
    x = s // (NC * NH)
    right = lo * NY + lax.rem(y + 1, NY)
    left = lo * NY + lax.rem(y + NY - 1, NY)
    pair = (1 - lo) * NY + y
    seqs = NX * NH * NC

    here = pl.ds(CAP, TOK)
    inputs = [
        pltpu.make_async_copy(tokens.at[0], xp.at[here], in_sem.at[0]),
        pltpu.make_async_copy(kwt, kw_in, in_sem.at[1]),
    ]
    for cp in inputs:
        cp.start()

    barrier = pltpu.get_barrier_semaphore()

    for dh, to_lo in ((0, lo), (1, lo), (3, lo), (3 - 2 * lo, 1 - lo), (2, 1 - lo)):
        def greet(i, _, dh=dh, to_lo=to_lo):
            t = (lax.rem(x + i // NC, NX) * NH + lax.rem(h + dh, NH)) * NC + lax.rem(c + lax.rem(i, NC), NC)
            pl.semaphore_signal(barrier, inc=1, device_id=(to_lo * NY + y, t), device_id_type=MESH)
            return 0

        lax.fori_loop(1 if isinstance(dh, int) and dh == 0 else 0, NX * NC, greet, 0)
    for t in (pair, left, right):
        pl.semaphore_signal(barrier, inc=1, device_id=(t, s), device_id_type=MESH)
    pl.semaphore_wait(barrier, 5 * NX * NC - 1 + 3)

    def remote(src, dst, ss, rs, blk, seq):
        return pltpu.make_async_remote_copy(
            src_ref=src, dst_ref=dst, send_sem=ss, recv_sem=rs, device_id=(blk, seq), device_id_type=MESH
        )

    def g_view(slot):
        return gu.at[slot, :, pl.ds(0, PIECE)]

    def u_view(slot):
        return gu.at[slot, :, pl.ds(PIECE, PIECE)]

    def d_view(slot, start, size):
        return wd.at[pl.ds(start, size), pl.ds(slot * PIECE, PIECE)]

    def view(a, slot):
        return (g_view, u_view)[a](slot) if a < 2 else d_view(slot, (a - 2) * BLOCK, BLOCK)

    def owned(a):
        return (gate_w, up_w)[a].at[0] if a < 2 else down_w.at[0, pl.ds((a - 2) * BLOCK, BLOCK)]

    def hop(way, step, a):
        slots = (LEFT, RIGHT)[way]
        if step == 4 and a >= 2:
            start = (a - 2) * BLOCK + way * BLOCK // 2
            src, dst = d_view(slots[3], start, BLOCK // 2), d_view(FAR, start, BLOCK // 2)
        else:
            src = owned(a) if step == 1 else view(a, slots[step - 1])
            dst = view(a, slots[step])
        return remote(src, dst, ag_s.at[way, step - 1, a], ag_r.at[way, step - 1, a], (right, left)[way], s)

    hops = []

    def send(step, a):
        for way in range(2):
            cp = hop(way, step, a)
            cp.start()
            hops.append(cp)

    def forward(step, a):
        for way in range(2):
            hop(way, step, a).wait_recv()
            if step < 3 or a >= 2 or a == way:
                cp = hop(way, step + 1, a)
                cp.start()
                hops.append(cp)

    tail = remote(tokens.at[0, pl.ds(TOK - CAP, CAP)], xp.at[pl.ds(0, CAP)], halo_s.at[0], halo_r.at[0], b, lax.rem(s + 1, seqs))
    head = remote(tokens.at[0, pl.ds(0, CAP)], xp.at[pl.ds(TOK + CAP, CAP)], halo_s.at[1], halo_r.at[1], b, lax.rem(s + seqs - 1, seqs))
    tail.start()
    head.start()
    send(1, 0)
    send(1, 1)
    send(1, 2)
    locals_ = [
        pltpu.make_async_copy(owned(a), view(a, OWN), local_sem.at[a]) for a in range(2 + BLOCKS)
    ]
    for cp in locals_:
        cp.start()

    xp[pl.ds(TOK + 2 * CAP, 32)] = jnp.zeros((32, D), BF16)
    row, col = iota((512, HEADS * TAPS), 0), iota((512, HEADS * TAPS), 1)
    tap = row & 31
    spread = ((col == (row >> 5) * TAPS + tap) & (tap < TAPS)).astype(F32).astype(BF16)
    for cp in inputs:
        cp.wait()
    kw = dot(spread, kw_in[...]).astype(BF16)
    for q in range(4):
        logits = dot_nt(kw[q * 128 : (q + 1) * 128], xp[here]).reshape(4, 32, TOK)
        logits = jnp.where(iota(logits.shape, 1) < TAPS, logits, -3e38)
        e = jnp.exp(logits - jnp.max(logits, axis=1, keepdims=True))
        p = e / jnp.sum(e, axis=1, keepdims=True)
        pt[q] = p.astype(BF16).astype(F32).reshape(128, TOK).T

    tail.wait_recv()
    head.wait_recv()
    first, last = (s > 0).astype(F32), (s < seqs - 1).astype(F32)
    xp[pl.ds(0, CAP)] = (xp[pl.ds(0, CAP)].astype(F32) * first).astype(BF16)
    xp[pl.ds(TOK + CAP, CAP)] = (xp[pl.ds(TOK + CAP, CAP)].astype(F32) * last).astype(BF16)

    lane = iota((64, 128), 1)
    for q in range(4):
        for t in range(TOK // 64):
            p = pt[q, pl.ds(t * 64, 64)]
            bands = []
            for i in range(4):
                mine_only = jnp.where((lane >> 5) == i, p, 0.0)
                bands.append(
                    pltpu.roll(mine_only, (1 - 32 * i) % 128, 1, stride=1, stride_axis=0).astype(BF16)
                )
            for i in range(2):
                cols = pl.ds((2 * q + i) * 128, 128)
                window = xp[pl.ds(t * 64, 128), cols]
                conv = jnp.where(lane < 64, dot(bands[2 * i], window), dot(bands[2 * i + 1], window))
                mixed[pl.ds(t * 64, 64), cols] = conv + xp[pl.ds(CAP + t * 64, 64), cols].astype(F32)

    m = mixed[...]
    scale = lax.rsqrt(jnp.mean(m * m, axis=1, keepdims=True) + EPS)
    normed[...] = (m * scale * gain[...].reshape(1, D).astype(F32)).astype(BF16)
    same = (iota((TOK, TOK), 0) == iota((TOK, TOK), 1)).astype(F32)
    idr = ids[...].astype(F32)
    idc = jnp.sum(same * idr, axis=1, keepdims=True)
    capr = limits[...].astype(F32)
    capc = jnp.sum(same[:EXPERTS, :EXPERTS] * capr, axis=1, keepdims=True)
    fc = (idc == iota((TOK, EXPERTS), 1).astype(F32)).astype(F32)
    fr = (idr == iota((EXPERTS, TOK), 0).astype(F32)).astype(F32)
    up_tri = (iota((TOK, TOK), 0) < iota((TOK, TOK), 1)).astype(F32).astype(BF16)
    lo_tri = (iota((TOK, TOK), 0) > iota((TOK, TOK), 1)).astype(F32).astype(BF16)
    rank_c = jnp.sum(dot(lo_tri, fc.astype(BF16)) * fc, axis=1, keepdims=True)
    rank_r = jnp.sum(dot(fr.astype(BF16), up_tri) * fr, axis=0, keepdims=True)
    cap_c = jnp.sum(fc * capr, axis=1, keepdims=True)
    cap_r = jnp.sum(fr * capc, axis=0, keepdims=True)
    slot_c = jnp.where(rank_c < cap_c, idc * CAP + rank_c, -1.0)
    slot_r = jnp.where(rank_r < cap_r, idr * CAP + rank_r, -1.0)
    sel[...] = (slot_c == iota((TOK, SLOTS), 1).astype(F32)).astype(F32).astype(BF16)
    sel_t = (slot_r == iota((SLOTS, TOK), 0).astype(F32)).astype(F32).astype(BF16)
    chosen = jnp.sum(dot_nt(normed[...], router[...]) * fc, axis=1, keepdims=True)
    gate_s[...] = 1.0 / (1.0 + jnp.exp(-chosen))
    packed[...] = dot(sel_t, normed[...]).astype(BF16)

    def aligned(v):
        return pl.multiple_of(v, CAP)

    def place(dx, kind, core):
        return aligned(dx * GROUP + (kind * NC + core) * CAP)

    def home(dh):
        return ((lo, 0), (0, 1 + lo), (1 - lo, 3), (1, 1 + lo))[dh]

    for dx in range(NX):
        def to(n, _, dx=dx, turns=(2, 1, 3, 0)):
            for dh in turns:
                home_lo, kind = home(dh)
                e = (lax.rem(x + dx, NX) * NH + lax.rem(h + dh, NH)) * NC + lax.rem(c + n, NC)
                remote(
                    packed.at[pl.ds(aligned(e * CAP), CAP)],
                    rows.at[pl.ds(place(dx, kind, c), CAP)],
                    fwd_s, fwd_r.at[dx], home_lo * NY + y, e,
                ).start()
            return 0

        if dx == 0:
            to(0, 0, turns=(2, 1, 3))
        lax.fori_loop(1 if dx == 0 else 0, NC, to, 0)
    rows[pl.ds(place(0, 0, c), CAP)] = packed[pl.ds(aligned(s * CAP), CAP)]

    ex = []

    def exchange(kind):
        n = GROUP - CAP if kind == 0 else GROUP
        block = rows.at[pl.ds(0, n)]
        remote(block, block, fwd_s, fwd_r.at[kind], b, s).wait_recv()
        src = rows.at[pl.ds(kind * GROUP, GROUP)]
        dst = rows.at[pl.ds(SLOTS + kind * GROUP, GROUP)]
        cp = remote(src, dst, ex_s.at[kind], ex_r.at[kind], pair, s)
        cp.start()
        ex.append(cp)

    def units(blocks, *slots):
        for slot in slots:
            for k in blocks:
                r = pl.ds(k * HALF_ROWS, HALF_ROWS)
                v = dot(rows[r], gu[slot])
                g, u = v[:, :PIECE], v[:, PIECE:]
                act[r, pl.ds(slot * PIECE, PIECE)] = (g / (1.0 + jnp.exp(-g)) * u).astype(BF16)

    forward(1, 0)
    forward(1, 1)
    forward(1, 2)
    exchange(0)
    for cp in locals_:
        cp.wait()
    forward(2, 0)
    forward(2, 1)
    forward(2, 2)
    send(1, 3)
    exchange(1)
    units((0,), 0, 1, 4, 2, 5)
    exchange(2)
    exchange(3)
    forward(3, 0)
    forward(3, 1)
    forward(3, 2)
    forward(1, 3)
    units((1,), 0, 1, 4, 2, 5)
    units((0, 1), 3, 6)
    ex[0].wait_recv()
    ex[1].wait_recv()
    send(1, 4)
    units((2,), 0, 1, 4, 2, 5, 3, 6)
    ex[2].wait_recv()
    ex[3].wait_recv()
    units((3,), 0, 1, 4, 2, 5, 3, 6)
    hop(0, 4, 0).wait_recv()
    hop(1, 4, 1).wait_recv()
    forward(2, 3)
    send(1, 5)
    units((3, 1, 2, 0), 7)

    order = [(j, i) for j in range(PARTS) for i in (1, 0)]

    def down(k, j):
        return dot_nt(act[pl.ds(k * HALF_ROWS, HALF_ROWS)], wd[pl.ds(j * FEAT, FEAT)])

    def part_of(ref, j, i):
        return ref.at[j, pl.ds(i * HALF_ROWS, HALF_ROWS)]

    px = [
        remote(part_of(ps, j, i), part_of(pr, j, i), px_s.at[n], px_r.at[n], pair, s)
        for n, (j, i) in enumerate(order)
    ]
    near = lax.rem(h + NH - 1 + 2 * lo, NH)

    def give(j, i):
        r = pl.ds(i * HALF_ROWS, HALF_ROWS)
        bs[j, r] = (mine[j, r] + pr[j, r].astype(F32)).astype(BF16)

        def back(n, _, kinds=(3, 1, 2, 0)):
            dx, tc = 2 * i + n // NC, lax.rem(c + lax.rem(n, NC), NC)
            for kind in kinds:
                to_h = (h, near, near, lax.rem(h + 2, NH))[kind]
                to_lo = (lo, 0, 1, 1 - lo)[kind]
                t = (lax.rem(x + NX - dx, NX) * NH + to_h) * NC + tc
                remote(
                    bs.at[j, pl.ds(place(dx, kind, tc), CAP)],
                    bk.at[j, pl.ds(aligned(s * CAP), CAP)],
                    ret_s.at[j], ret_r.at[j], to_lo * NY + y, t,
                ).start()
            return 0

        if i == 0:
            back(0, 0, kinds=(3, 1, 2))
            bk[j, pl.ds(aligned(s * CAP), CAP)] = bs[j, pl.ds(place(0, 0, c), CAP)]
        lax.fori_loop(1 if i == 0 else 0, 2 * NC, back, 0)

    def arrived(a):
        for way in range(2):
            hop(way, 4, a).wait_recv()

    passing = {0: ((3, 3), (1, 4)), 1: ((2, 4), (1, 5)), 2: ((3, 4), (2, 5)), 3: ((3, 5),)}
    for n, (j, i) in enumerate(order):
        if n % 2 == 0:
            arrived(2 + j * BLOCKS // PARTS)
        r = pl.ds(i * HALF_ROWS, HALF_ROWS)
        ps[j, r] = down(2 + i, j).astype(BF16)
        if n >= AHEAD:
            px[n - AHEAD].wait_recv()
        px[n].start()
        mine[j, r] = down(i, j)
        if n >= AHEAD:
            give(*order[n - AHEAD])
        for step, a in passing.get(n, ()):
            forward(step, a)
    for n in range(len(order) - AHEAD, len(order)):
        px[n].wait_recv()
        give(*order[n])

    for j in range(PARTS):
        block = bk.at[j, pl.ds(0, SLOTS - CAP)]
        remote(block, block, ret_s.at[j], ret_r.at[j], b, s).wait_recv()
        cols = pl.ds(j * FEAT, FEAT)
        out[0, :, cols] = (mixed[:, cols] + gate_s[...] * dot(sel[...], bk[j])).astype(BF16)

    tail.wait_send()
    head.wait_send()
    for cp in hops + ex + px:
        cp.wait_send()
    block = packed.at[pl.ds(0, SLOTS - CAP)]
    remote(block, block, fwd_s, fwd_r.at[0], b, s).wait_send()
    for j in range(PARTS):
        block = bs.at[j, pl.ds(0, SLOTS - CAP)]
        remote(block, block, ret_s.at[j], ret_r.at[j], b, s).wait_send()


def on_device(tokens, expert_ids, expert_capacity, kernel_weight, norm_gain, router, expert_gate, expert_up, expert_down):
    dma = pltpu.SemaphoreType.DMA
    vmem = pl.BlockSpec(memory_space=pltpu.VMEM)
    anywhere = pl.BlockSpec(memory_space=pl.ANY)
    return pl.pallas_call(
        layer,
        out_shape=jax.ShapeDtypeStruct((1, TOK, D), BF16),
        in_specs=[anywhere, vmem, vmem, anywhere, vmem, vmem] + [anywhere] * 3,
        out_specs=vmem,
        scratch_shapes=[
            pltpu.VMEM((TOK + 4 * CAP, D), BF16),
            pltpu.VMEM((HEADS * TAPS, D), BF16),
            pltpu.VMEM((4, TOK, 128), F32),
            pltpu.VMEM((TOK, D), F32),
            pltpu.VMEM((TOK, D), BF16),
            pltpu.VMEM((SLOTS, D), BF16),
            pltpu.VMEM((TOK, SLOTS), BF16),
            pltpu.VMEM((TOK, 1), F32),
            pltpu.VMEM((2 * SLOTS, D), BF16),
            pltpu.VMEM((NY, D, 2 * PIECE), BF16),
            pltpu.VMEM((D, NY * PIECE), BF16),
            pltpu.VMEM((2 * SLOTS, NY * PIECE), BF16),
            pltpu.VMEM((PARTS, SLOTS, FEAT), BF16),
            pltpu.VMEM((PARTS, SLOTS, FEAT), BF16),
            pltpu.VMEM((PARTS, SLOTS, FEAT), F32),
            pltpu.VMEM((PARTS, SLOTS, FEAT), BF16),
            pltpu.VMEM((PARTS, SLOTS, FEAT), BF16),
            dma((2,)),
            dma((2 + BLOCKS,)),
            dma((2,)), dma((2,)),
            dma((2, 4, 2 + BLOCKS)), dma((2, 4, 2 + BLOCKS)),
            dma, dma((4,)),
            dma((4,)), dma((4,)),
            dma((2 * PARTS,)), dma((2 * PARTS,)),
            dma((PARTS,)), dma((PARTS,)),
        ],
        compiler_params=pltpu.CompilerParams(
            collective_id=0, has_side_effects=True, vmem_limit_bytes=56 * 1024 * 1024
        ),
    )(
        tokens,
        expert_ids.reshape(1, TOK),
        expert_capacity.reshape(1, EXPERTS),
        kernel_weight.T,
        norm_gain,
        router.T,
        expert_gate,
        expert_up,
        expert_down,
    )


def solution(mesh):
    placed = (
        P("blk", "seq", None),
        P("blk", "seq", None),
        P(),
        P(),
        P(),
        P(),
        P("seq", None, "blk"),
        P("seq", None, "blk"),
        P("seq", None, "blk"),
    )
    return jax.shard_map(
        on_device, mesh=mesh, in_specs=placed, out_specs=P("blk", "seq", None), check_vma=False
    )
```

```python
import functools

import jax
import jax.numpy as jnp
from jax import lax
from jax.experimental import pallas as pl
from jax.experimental.pallas import tpu as pltpu
from jax.sharding import PartitionSpec as P

MESH = pl.DeviceIdType.MESH
F32 = jnp.float32
BF16 = jnp.bfloat16

D = 1024
HEADS = 16
TAPS = 31
HALF = 15
TOK = 256
EXPERTS = 32
CAP = 16
SLOTS = EXPERTS * CAP
EPS = 1e-06

NX, NH, NC, NY = 4, 4, 2, 8
GROUP = NH * NC * CAP
PIECE = 128
PARTS = 4
FEAT = D // PARTS
BLOCKS = 4
BLOCK = D // BLOCKS
HALF_ROWS = SLOTS // 2
AHEAD = 2

OWN, FAR = 0, 7
LEFT = (0, 1, 2, 3, 7)
RIGHT = (0, 4, 5, 6, 7)


def dot(a, b):
    return jnp.dot(a, b, preferred_element_type=F32)


def dot_nt(a, b):
    return lax.dot_general(a, b, (((1,), (1,)), ((), ())), preferred_element_type=F32)


def iota(shape, dim):
    return lax.broadcasted_iota(jnp.int32, shape, dim)


def layer(
    tokens, ids, limits, kwt, gain, router, gate_w, up_w, down_w,
    out,
    xp, kw_in, pt, mixed, normed, packed, sel, gate_s,
    rows, gu, wd, act, ps, pr, mine, bs, bk,
    in_sem, local_sem, halo_s, halo_r, ag_s, ag_r, fwd_s, fwd_r, ex_s, ex_r, px_s, px_r, ret_s, ret_r,
):
    s = lax.axis_index("seq")
    b = lax.axis_index("blk")
    lo, y = b // NY, lax.rem(b, NY)
    c = lax.rem(s, NC)
    h = lax.rem(s // NC, NH)
    x = s // (NC * NH)
    right = lo * NY + lax.rem(y + 1, NY)
    left = lo * NY + lax.rem(y + NY - 1, NY)
    pair = (1 - lo) * NY + y
    seqs = NX * NH * NC

    here = pl.ds(CAP, TOK)
    inputs = [
        pltpu.make_async_copy(tokens.at[0], xp.at[here], in_sem.at[0]),
        pltpu.make_async_copy(kwt, kw_in, in_sem.at[1]),
    ]
    for cp in inputs:
        cp.start()

    barrier = pltpu.get_barrier_semaphore()

    for dh, to_lo in ((0, lo), (1, lo), (3, lo), (3 - 2 * lo, 1 - lo), (2, 1 - lo)):
        def greet(i, _, dh=dh, to_lo=to_lo):
            t = (lax.rem(x + i // NC, NX) * NH + lax.rem(h + dh, NH)) * NC + lax.rem(c + lax.rem(i, NC), NC)
            pl.semaphore_signal(barrier, inc=1, device_id=(to_lo * NY + y, t), device_id_type=MESH)
            return 0

        lax.fori_loop(1 if isinstance(dh, int) and dh == 0 else 0, NX * NC, greet, 0)
    for t in (pair, left, right):
        pl.semaphore_signal(barrier, inc=1, device_id=(t, s), device_id_type=MESH)
    pl.semaphore_wait(barrier, 5 * NX * NC - 1 + 3)

    def remote(src, dst, ss, rs, blk, seq):
        return pltpu.make_async_remote_copy(
            src_ref=src, dst_ref=dst, send_sem=ss, recv_sem=rs, device_id=(blk, seq), device_id_type=MESH
        )

    def g_view(slot):
        return gu.at[slot, :, pl.ds(0, PIECE)]

    def u_view(slot):
        return gu.at[slot, :, pl.ds(PIECE, PIECE)]

    def d_view(slot, start, size):
        return wd.at[pl.ds(start, size), pl.ds(slot * PIECE, PIECE)]

    def view(a, slot):
        return (g_view, u_view)[a](slot) if a < 2 else d_view(slot, (a - 2) * BLOCK, BLOCK)

    def owned(a):
        return (gate_w, up_w)[a].at[0] if a < 2 else down_w.at[0, pl.ds((a - 2) * BLOCK, BLOCK)]

    def hop(way, step, a):
        slots = (LEFT, RIGHT)[way]
        if step == 4 and a >= 2:
            start = (a - 2) * BLOCK + way * BLOCK // 2
            src, dst = d_view(slots[3], start, BLOCK // 2), d_view(FAR, start, BLOCK // 2)
        else:
            src = owned(a) if step == 1 else view(a, slots[step - 1])
            dst = view(a, slots[step])
        return remote(src, dst, ag_s.at[way, step - 1, a], ag_r.at[way, step - 1, a], (right, left)[way], s)

    hops = []

    def send(step, a):
        for way in range(2):
            cp = hop(way, step, a)
            cp.start()
            hops.append(cp)

    def forward(step, a):
        for way in range(2):
            hop(way, step, a).wait_recv()
            if step < 3 or a >= 2 or a == way:
                cp = hop(way, step + 1, a)
                cp.start()
                hops.append(cp)

    tail = remote(tokens.at[0, pl.ds(TOK - CAP, CAP)], xp.at[pl.ds(0, CAP)], halo_s.at[0], halo_r.at[0], b, lax.rem(s + 1, seqs))
    head = remote(tokens.at[0, pl.ds(0, CAP)], xp.at[pl.ds(TOK + CAP, CAP)], halo_s.at[1], halo_r.at[1], b, lax.rem(s + seqs - 1, seqs))
    tail.start()
    head.start()
    send(1, 0)
    send(1, 1)
    send(1, 2)
    locals_ = [
        pltpu.make_async_copy(owned(a), view(a, OWN), local_sem.at[a]) for a in range(2 + BLOCKS)
    ]
    for cp in locals_:
        cp.start()

    xp[pl.ds(TOK + 2 * CAP, 32)] = jnp.zeros((32, D), BF16)
    row, col = iota((512, HEADS * TAPS), 0), iota((512, HEADS * TAPS), 1)
    tap = row & 31
    spread = ((col == (row >> 5) * TAPS + tap) & (tap < TAPS)).astype(F32).astype(BF16)
    for cp in inputs:
        cp.wait()
    kw = dot(spread, kw_in[...]).astype(BF16)
    for q in range(4):
        logits = dot_nt(kw[q * 128 : (q + 1) * 128], xp[here]).reshape(4, 32, TOK)
        logits = jnp.where(iota(logits.shape, 1) < TAPS, logits, -3e38)
        e = jnp.exp(logits - jnp.max(logits, axis=1, keepdims=True))
        p = e / jnp.sum(e, axis=1, keepdims=True)
        pt[q] = p.astype(BF16).astype(F32).reshape(128, TOK).T

    tail.wait_recv()
    head.wait_recv()
    first, last = (s > 0).astype(F32), (s < seqs - 1).astype(F32)
    xp[pl.ds(0, CAP)] = (xp[pl.ds(0, CAP)].astype(F32) * first).astype(BF16)
    xp[pl.ds(TOK + CAP, CAP)] = (xp[pl.ds(TOK + CAP, CAP)].astype(F32) * last).astype(BF16)

    lane = iota((64, 128), 1)
    for q in range(4):
        for t in range(TOK // 64):
            p = pt[q, pl.ds(t * 64, 64)]
            bands = []
            for i in range(4):
                mine_only = jnp.where((lane >> 5) == i, p, 0.0)
                bands.append(
                    pltpu.roll(mine_only, (1 - 32 * i) % 128, 1, stride=1, stride_axis=0).astype(BF16)
                )
            for i in range(2):
                cols = pl.ds((2 * q + i) * 128, 128)
                window = xp[pl.ds(t * 64, 128), cols]
                conv = jnp.where(lane < 64, dot(bands[2 * i], window), dot(bands[2 * i + 1], window))
                mixed[pl.ds(t * 64, 64), cols] = conv + xp[pl.ds(CAP + t * 64, 64), cols].astype(F32)

    m = mixed[...]
    scale = lax.rsqrt(jnp.mean(m * m, axis=1, keepdims=True) + EPS)
    normed[...] = (m * scale * gain[...].reshape(1, D).astype(F32)).astype(BF16)
    same = (iota((TOK, TOK), 0) == iota((TOK, TOK), 1)).astype(F32)
    idr = ids[...].astype(F32)
    idc = jnp.sum(same * idr, axis=1, keepdims=True)
    capr = limits[...].astype(F32)
    capc = jnp.sum(same[:EXPERTS, :EXPERTS] * capr, axis=1, keepdims=True)
    fc = (idc == iota((TOK, EXPERTS), 1).astype(F32)).astype(F32)
    fr = (idr == iota((EXPERTS, TOK), 0).astype(F32)).astype(F32)
    up_tri = (iota((TOK, TOK), 0) < iota((TOK, TOK), 1)).astype(F32).astype(BF16)
    lo_tri = (iota((TOK, TOK), 0) > iota((TOK, TOK), 1)).astype(F32).astype(BF16)
    rank_c = jnp.sum(dot(lo_tri, fc.astype(BF16)) * fc, axis=1, keepdims=True)
    rank_r = jnp.sum(dot(fr.astype(BF16), up_tri) * fr, axis=0, keepdims=True)
    cap_c = jnp.sum(fc * capr, axis=1, keepdims=True)
    cap_r = jnp.sum(fr * capc, axis=0, keepdims=True)
    slot_c = jnp.where(rank_c < cap_c, idc * CAP + rank_c, -1.0)
    slot_r = jnp.where(rank_r < cap_r, idr * CAP + rank_r, -1.0)
    sel[...] = (slot_c == iota((TOK, SLOTS), 1).astype(F32)).astype(F32).astype(BF16)
    sel_t = (slot_r == iota((SLOTS, TOK), 0).astype(F32)).astype(F32).astype(BF16)
    chosen = jnp.sum(dot_nt(normed[...], router[...]) * fc, axis=1, keepdims=True)
    gate_s[...] = 1.0 / (1.0 + jnp.exp(-chosen))
    packed[...] = dot(sel_t, normed[...]).astype(BF16)

    def aligned(v):
        return pl.multiple_of(v, CAP)

    def place(dx, kind, core):
        return aligned(dx * GROUP + (kind * NC + core) * CAP)

    def home(dh):
        return ((lo, 0), (0, 1 + lo), (1 - lo, 3), (1, 1 + lo))[dh]

    for dx in range(NX):
        def to(n, _, dx=dx, turns=(2, 1, 3, 0)):
            for dh in turns:
                home_lo, kind = home(dh)
                e = (lax.rem(x + dx, NX) * NH + lax.rem(h + dh, NH)) * NC + lax.rem(c + n, NC)
                remote(
                    packed.at[pl.ds(aligned(e * CAP), CAP)],
                    rows.at[pl.ds(place(dx, kind, c), CAP)],
                    fwd_s, fwd_r.at[dx], home_lo * NY + y, e,
                ).start()
            return 0

        if dx == 0:
            to(0, 0, turns=(2, 1, 3))
        lax.fori_loop(1 if dx == 0 else 0, NC, to, 0)
    rows[pl.ds(place(0, 0, c), CAP)] = packed[pl.ds(aligned(s * CAP), CAP)]

    ex = []

    def exchange(kind):
        n = GROUP - CAP if kind == 0 else GROUP
        block = rows.at[pl.ds(0, n)]
        remote(block, block, fwd_s, fwd_r.at[kind], b, s).wait_recv()
        src = rows.at[pl.ds(kind * GROUP, GROUP)]
        dst = rows.at[pl.ds(SLOTS + kind * GROUP, GROUP)]
        cp = remote(src, dst, ex_s.at[kind], ex_r.at[kind], pair, s)
        cp.start()
        ex.append(cp)

    def units(blocks, *slots):
        for slot in slots:
            for k in blocks:
                r = pl.ds(k * HALF_ROWS, HALF_ROWS)
                v = dot(rows[r], gu[slot])
                g, u = v[:, :PIECE], v[:, PIECE:]
                act[r, pl.ds(slot * PIECE, PIECE)] = (g / (1.0 + jnp.exp(-g)) * u).astype(BF16)

    forward(1, 0)
    forward(1, 1)
    forward(1, 2)
    exchange(0)
    for cp in locals_:
        cp.wait()
    forward(2, 0)
    forward(2, 1)
    forward(2, 2)
    send(1, 3)
    exchange(1)
    units((0,), 0, 1, 4, 2, 5)
    exchange(2)
    exchange(3)
    forward(3, 0)
    forward(3, 1)
    forward(3, 2)
    forward(1, 3)
    units((1,), 0, 1, 4, 2, 5)
    units((0, 1), 3, 6)
    ex[0].wait_recv()
    ex[1].wait_recv()
    send(1, 4)
    units((2,), 0, 1, 4, 2, 5, 3, 6)
    ex[2].wait_recv()
    ex[3].wait_recv()
    units((3,), 0, 1, 4, 2, 5, 3, 6)
    hop(0, 4, 0).wait_recv()
    hop(1, 4, 1).wait_recv()
    forward(2, 3)
    send(1, 5)
    units((3, 1, 2, 0), 7)

    order = [(j, i) for j in range(PARTS) for i in (1, 0)]

    def down(k, j):
        return dot_nt(act[pl.ds(k * HALF_ROWS, HALF_ROWS)], wd[pl.ds(j * FEAT, FEAT)])

    def part_of(ref, j, i):
        return ref.at[j, pl.ds(i * HALF_ROWS, HALF_ROWS)]

    px = [
        remote(part_of(ps, j, i), part_of(pr, j, i), px_s.at[n], px_r.at[n], pair, s)
        for n, (j, i) in enumerate(order)
    ]
    near = lax.rem(h + NH - 1 + 2 * lo, NH)

    def give(j, i):
        r = pl.ds(i * HALF_ROWS, HALF_ROWS)
        bs[j, r] = (mine[j, r] + pr[j, r].astype(F32)).astype(BF16)

        def back(n, _, kinds=(3, 1, 2, 0)):
            dx, tc = 2 * i + n // NC, lax.rem(c + lax.rem(n, NC), NC)
            for kind in kinds:
                to_h = (h, near, near, lax.rem(h + 2, NH))[kind]
                to_lo = (lo, 0, 1, 1 - lo)[kind]
                t = (lax.rem(x + NX - dx, NX) * NH + to_h) * NC + tc
                remote(
                    bs.at[j, pl.ds(place(dx, kind, tc), CAP)],
                    bk.at[j, pl.ds(aligned(s * CAP), CAP)],
                    ret_s.at[j], ret_r.at[j], to_lo * NY + y, t,
                ).start()
            return 0

        if i == 0:
            back(0, 0, kinds=(3, 1, 2))
            bk[j, pl.ds(aligned(s * CAP), CAP)] = bs[j, pl.ds(place(0, 0, c), CAP)]
        lax.fori_loop(1 if i == 0 else 0, 2 * NC, back, 0)

    def arrived(a):
        for way in range(2):
            hop(way, 4, a).wait_recv()

    passing = {0: ((3, 3), (1, 4)), 1: ((2, 4), (1, 5)), 2: ((3, 4), (2, 5)), 3: ((3, 5),)}
    for n, (j, i) in enumerate(order):
        if n % 2 == 0:
            arrived(2 + j * BLOCKS // PARTS)
        r = pl.ds(i * HALF_ROWS, HALF_ROWS)
        ps[j, r] = down(2 + i, j).astype(BF16)
        if n >= AHEAD:
            px[n - AHEAD].wait_recv()
        px[n].start()
        if n >= AHEAD:
            give(*order[n - AHEAD])
        mine[j, r] = down(i, j)
        for step, a in passing.get(n, ()):
            forward(step, a)
    for n in range(len(order) - AHEAD, len(order)):
        px[n].wait_recv()
        give(*order[n])

    for j in range(PARTS):
        block = bk.at[j, pl.ds(0, SLOTS - CAP)]
        remote(block, block, ret_s.at[j], ret_r.at[j], b, s).wait_recv()
        cols = pl.ds(j * FEAT, FEAT)
        out[0, :, cols] = (mixed[:, cols] + gate_s[...] * dot(sel[...], bk[j])).astype(BF16)

    tail.wait_send()
    head.wait_send()
    for cp in hops + ex + px:
        cp.wait_send()
    block = packed.at[pl.ds(0, SLOTS - CAP)]
    remote(block, block, fwd_s, fwd_r.at[0], b, s).wait_send()
    for j in range(PARTS):
        block = bs.at[j, pl.ds(0, SLOTS - CAP)]
        remote(block, block, ret_s.at[j], ret_r.at[j], b, s).wait_send()


def on_device(tokens, expert_ids, expert_capacity, kernel_weight, norm_gain, router, expert_gate, expert_up, expert_down):
    dma = pltpu.SemaphoreType.DMA
    vmem = pl.BlockSpec(memory_space=pltpu.VMEM)
    anywhere = pl.BlockSpec(memory_space=pl.ANY)
    return pl.pallas_call(
        layer,
        out_shape=jax.ShapeDtypeStruct((1, TOK, D), BF16),
        in_specs=[anywhere, vmem, vmem, anywhere, vmem, vmem] + [anywhere] * 3,
        out_specs=vmem,
        scratch_shapes=[
            pltpu.VMEM((TOK + 4 * CAP, D), BF16),
            pltpu.VMEM((HEADS * TAPS, D), BF16),
            pltpu.VMEM((4, TOK, 128), F32),
            pltpu.VMEM((TOK, D), F32),
            pltpu.VMEM((TOK, D), BF16),
            pltpu.VMEM((SLOTS, D), BF16),
            pltpu.VMEM((TOK, SLOTS), BF16),
            pltpu.VMEM((TOK, 1), F32),
            pltpu.VMEM((2 * SLOTS, D), BF16),
            pltpu.VMEM((NY, D, 2 * PIECE), BF16),
            pltpu.VMEM((D, NY * PIECE), BF16),
            pltpu.VMEM((2 * SLOTS, NY * PIECE), BF16),
            pltpu.VMEM((PARTS, SLOTS, FEAT), BF16),
            pltpu.VMEM((PARTS, SLOTS, FEAT), BF16),
            pltpu.VMEM((PARTS, SLOTS, FEAT), F32),
            pltpu.VMEM((PARTS, SLOTS, FEAT), BF16),
            pltpu.VMEM((PARTS, SLOTS, FEAT), BF16),
            dma((2,)),
            dma((2 + BLOCKS,)),
            dma((2,)), dma((2,)),
            dma((2, 4, 2 + BLOCKS)), dma((2, 4, 2 + BLOCKS)),
            dma, dma((4,)),
            dma((4,)), dma((4,)),
            dma((2 * PARTS,)), dma((2 * PARTS,)),
            dma((PARTS,)), dma((PARTS,)),
        ],
        compiler_params=pltpu.CompilerParams(
            collective_id=0, has_side_effects=True, vmem_limit_bytes=56 * 1024 * 1024
        ),
    )(
        tokens,
        expert_ids.reshape(1, TOK),
        expert_capacity.reshape(1, EXPERTS),
        kernel_weight.T,
        norm_gain,
        router.T,
        expert_gate,
        expert_up,
        expert_down,
    )


def solution(mesh):
    placed = (
        P("blk", "seq", None),
        P("blk", "seq", None),
        P(),
        P(),
        P(),
        P(),
        P("seq", None, "blk"),
        P("seq", None, "blk"),
        P("seq", None, "blk"),
    )
    return jax.shard_map(
        on_device, mesh=mesh, in_specs=placed, out_specs=P("blk", "seq", None), check_vma=False
    )
```

```python
import functools

import jax
import jax.numpy as jnp
from jax import lax
from jax.experimental import pallas as pl
from jax.experimental.pallas import tpu as pltpu
from jax.sharding import PartitionSpec as P

MESH = pl.DeviceIdType.MESH
F32 = jnp.float32
BF16 = jnp.bfloat16

D = 1024
HEADS = 16
TAPS = 31
HALF = 15
TOK = 256
EXPERTS = 32
CAP = 16
SLOTS = EXPERTS * CAP
EPS = 1e-06

NX, NH, NC, NY = 4, 4, 2, 8
GROUP = NH * NC * CAP
PIECE = 128
PARTS = 4
FEAT = D // PARTS
BLOCKS = 4
BLOCK = D // BLOCKS
HALF_ROWS = SLOTS // 2
AHEAD = 2

OWN, FAR = 0, 7
LEFT = (0, 1, 2, 3, 7)
RIGHT = (0, 4, 5, 6, 7)


def dot(a, b):
    return jnp.dot(a, b, preferred_element_type=F32)


def dot_nt(a, b):
    return lax.dot_general(a, b, (((1,), (1,)), ((), ())), preferred_element_type=F32)


def iota(shape, dim):
    return lax.broadcasted_iota(jnp.int32, shape, dim)


def layer(
    tokens, ids, limits, kwt, gain, router, gate_w, up_w, down_w,
    out,
    xp, kw_in, pt, mixed, normed, packed, sel, gate_s,
    rows, gu, wd, act, ps, pr, mine, bs, bk,
    in_sem, local_sem, halo_s, halo_r, ag_s, ag_r, fwd_s, fwd_r, ex_s, ex_r, px_s, px_r, ret_s, ret_r,
):
    s = lax.axis_index("seq")
    b = lax.axis_index("blk")
    lo, y = b // NY, lax.rem(b, NY)
    c = lax.rem(s, NC)
    h = lax.rem(s // NC, NH)
    x = s // (NC * NH)
    right = lo * NY + lax.rem(y + 1, NY)
    left = lo * NY + lax.rem(y + NY - 1, NY)
    pair = (1 - lo) * NY + y
    seqs = NX * NH * NC

    here = pl.ds(CAP, TOK)
    inputs = [
        pltpu.make_async_copy(tokens.at[0], xp.at[here], in_sem.at[0]),
        pltpu.make_async_copy(kwt, kw_in, in_sem.at[1]),
    ]
    for cp in inputs:
        cp.start()

    barrier = pltpu.get_barrier_semaphore()

    for dh, to_lo in ((0, lo), (1, lo), (3, lo), (3 - 2 * lo, 1 - lo), (2, 1 - lo)):
        def greet(i, _, dh=dh, to_lo=to_lo):
            t = (lax.rem(x + i // NC, NX) * NH + lax.rem(h + dh, NH)) * NC + lax.rem(c + lax.rem(i, NC), NC)
            pl.semaphore_signal(barrier, inc=1, device_id=(to_lo * NY + y, t), device_id_type=MESH)
            return 0

        lax.fori_loop(1 if isinstance(dh, int) and dh == 0 else 0, NX * NC, greet, 0)
    for t in (pair, left, right):
        pl.semaphore_signal(barrier, inc=1, device_id=(t, s), device_id_type=MESH)
    pl.semaphore_wait(barrier, 5 * NX * NC - 1 + 3)

    def remote(src, dst, ss, rs, blk, seq):
        return pltpu.make_async_remote_copy(
            src_ref=src, dst_ref=dst, send_sem=ss, recv_sem=rs, device_id=(blk, seq), device_id_type=MESH
        )

    def g_view(slot):
        return gu.at[slot, :, pl.ds(0, PIECE)]

    def u_view(slot):
        return gu.at[slot, :, pl.ds(PIECE, PIECE)]

    def d_view(slot, start, size):
        return wd.at[pl.ds(start, size), pl.ds(slot * PIECE, PIECE)]

    def view(a, slot):
        return (g_view, u_view)[a](slot) if a < 2 else d_view(slot, (a - 2) * BLOCK, BLOCK)

    def owned(a):
        return (gate_w, up_w)[a].at[0] if a < 2 else down_w.at[0, pl.ds((a - 2) * BLOCK, BLOCK)]

    def hop(way, step, a):
        slots = (LEFT, RIGHT)[way]
        if step == 4 and a >= 2:
            start = (a - 2) * BLOCK + way * BLOCK // 2
            src, dst = d_view(slots[3], start, BLOCK // 2), d_view(FAR, start, BLOCK // 2)
        else:
            src = owned(a) if step == 1 else view(a, slots[step - 1])
            dst = view(a, slots[step])
        return remote(src, dst, ag_s.at[way, step - 1, a], ag_r.at[way, step - 1, a], (right, left)[way], s)

    hops = []

    def send(step, a):
        for way in range(2):
            cp = hop(way, step, a)
            cp.start()
            hops.append(cp)

    def forward(step, a):
        for way in range(2):
            hop(way, step, a).wait_recv()
            if step < 3 or a >= 2 or a == way:
                cp = hop(way, step + 1, a)
                cp.start()
                hops.append(cp)

    tail = remote(tokens.at[0, pl.ds(TOK - CAP, CAP)], xp.at[pl.ds(0, CAP)], halo_s.at[0], halo_r.at[0], b, lax.rem(s + 1, seqs))
    head = remote(tokens.at[0, pl.ds(0, CAP)], xp.at[pl.ds(TOK + CAP, CAP)], halo_s.at[1], halo_r.at[1], b, lax.rem(s + seqs - 1, seqs))
    tail.start()
    head.start()
    send(1, 0)
    send(1, 1)
    send(1, 2)
    locals_ = [
        pltpu.make_async_copy(owned(a), view(a, OWN), local_sem.at[a]) for a in range(2 + BLOCKS)
    ]
    for cp in locals_:
        cp.start()

    xp[pl.ds(TOK + 2 * CAP, 32)] = jnp.zeros((32, D), BF16)
    row, col = iota((512, HEADS * TAPS), 0), iota((512, HEADS * TAPS), 1)
    tap = row & 31
    spread = ((col == (row >> 5) * TAPS + tap) & (tap < TAPS)).astype(F32).astype(BF16)
    for cp in inputs:
        cp.wait()
    kw = dot(spread, kw_in[...]).astype(BF16)
    for q in range(4):
        logits = dot_nt(kw[q * 128 : (q + 1) * 128], xp[here]).reshape(4, 32, TOK)
        logits = jnp.where(iota(logits.shape, 1) < TAPS, logits, -3e38)
        e = jnp.exp(logits - jnp.max(logits, axis=1, keepdims=True))
        p = e / jnp.sum(e, axis=1, keepdims=True)
        pt[q] = p.astype(BF16).astype(F32).reshape(128, TOK).T

    tail.wait_recv()
    head.wait_recv()
    first, last = (s > 0).astype(F32), (s < seqs - 1).astype(F32)
    xp[pl.ds(0, CAP)] = (xp[pl.ds(0, CAP)].astype(F32) * first).astype(BF16)
    xp[pl.ds(TOK + CAP, CAP)] = (xp[pl.ds(TOK + CAP, CAP)].astype(F32) * last).astype(BF16)

    lane = iota((64, 128), 1)
    for q in range(4):
        for t in range(TOK // 64):
            p = pt[q, pl.ds(t * 64, 64)]
            bands = []
            for i in range(4):
                mine_only = jnp.where((lane >> 5) == i, p, 0.0)
                bands.append(
                    pltpu.roll(mine_only, (1 - 32 * i) % 128, 1, stride=1, stride_axis=0).astype(BF16)
                )
            for i in range(2):
                cols = pl.ds((2 * q + i) * 128, 128)
                window = xp[pl.ds(t * 64, 128), cols]
                conv = jnp.where(lane < 64, dot(bands[2 * i], window), dot(bands[2 * i + 1], window))
                mixed[pl.ds(t * 64, 64), cols] = conv + xp[pl.ds(CAP + t * 64, 64), cols].astype(F32)

    m = mixed[...]
    scale = lax.rsqrt(jnp.mean(m * m, axis=1, keepdims=True) + EPS)
    normed[...] = (m * scale * gain[...].reshape(1, D).astype(F32)).astype(BF16)
    same = (iota((TOK, TOK), 0) == iota((TOK, TOK), 1)).astype(F32)
    idr = ids[...].astype(F32)
    idc = jnp.sum(same * idr, axis=1, keepdims=True)
    capr = limits[...].astype(F32)
    capc = jnp.sum(same[:EXPERTS, :EXPERTS] * capr, axis=1, keepdims=True)
    fc = (idc == iota((TOK, EXPERTS), 1).astype(F32)).astype(F32)
    fr = (idr == iota((EXPERTS, TOK), 0).astype(F32)).astype(F32)
    up_tri = (iota((TOK, TOK), 0) < iota((TOK, TOK), 1)).astype(F32).astype(BF16)
    lo_tri = (iota((TOK, TOK), 0) > iota((TOK, TOK), 1)).astype(F32).astype(BF16)
    rank_c = jnp.sum(dot(lo_tri, fc.astype(BF16)) * fc, axis=1, keepdims=True)
    rank_r = jnp.sum(dot(fr.astype(BF16), up_tri) * fr, axis=0, keepdims=True)
    cap_c = jnp.sum(fc * capr, axis=1, keepdims=True)
    cap_r = jnp.sum(fr * capc, axis=0, keepdims=True)
    slot_c = jnp.where(rank_c < cap_c, idc * CAP + rank_c, -1.0)
    slot_r = jnp.where(rank_r < cap_r, idr * CAP + rank_r, -1.0)
    sel[...] = (slot_c == iota((TOK, SLOTS), 1).astype(F32)).astype(F32).astype(BF16)
    sel_t = (slot_r == iota((SLOTS, TOK), 0).astype(F32)).astype(F32).astype(BF16)
    chosen = jnp.sum(dot_nt(normed[...], router[...]) * fc, axis=1, keepdims=True)
    gate_s[...] = 1.0 / (1.0 + jnp.exp(-chosen))
    packed[...] = dot(sel_t, normed[...]).astype(BF16)

    def aligned(v):
        return pl.multiple_of(v, CAP)

    def place(dx, kind, core):
        return aligned(dx * GROUP + (kind * NC + core) * CAP)

    def home(dh):
        return ((lo, 0), (0, 1 + lo), (1 - lo, 3), (1, 1 + lo))[dh]

    for dx in range(NX):
        def to(n, _, dx=dx, turns=(2, 1, 3, 0)):
            for dh in turns:
                home_lo, kind = home(dh)
                e = (lax.rem(x + dx, NX) * NH + lax.rem(h + dh, NH)) * NC + lax.rem(c + n, NC)
                remote(
                    packed.at[pl.ds(aligned(e * CAP), CAP)],
                    rows.at[pl.ds(place(dx, kind, c), CAP)],
                    fwd_s, fwd_r.at[dx], home_lo * NY + y, e,
                ).start()
            return 0

        if dx == 0:
            to(0, 0, turns=(2, 1, 3))
        lax.fori_loop(1 if dx == 0 else 0, NC, to, 0)
    rows[pl.ds(place(0, 0, c), CAP)] = packed[pl.ds(aligned(s * CAP), CAP)]

    ex = []

    def exchange(kind):
        n = GROUP - CAP if kind == 0 else GROUP
        block = rows.at[pl.ds(0, n)]
        remote(block, block, fwd_s, fwd_r.at[kind], b, s).wait_recv()
        src = rows.at[pl.ds(kind * GROUP, GROUP)]
        dst = rows.at[pl.ds(SLOTS + kind * GROUP, GROUP)]
        cp = remote(src, dst, ex_s.at[kind], ex_r.at[kind], pair, s)
        cp.start()
        ex.append(cp)

    def units(blocks, *slots):
        for slot in slots:
            for k in blocks:
                r = pl.ds(k * HALF_ROWS, HALF_ROWS)
                v = dot(rows[r], gu[slot])
                g, u = v[:, :PIECE], v[:, PIECE:]
                act[r, pl.ds(slot * PIECE, PIECE)] = (g / (1.0 + jnp.exp(-g)) * u).astype(BF16)

    forward(1, 0)
    forward(1, 1)
    forward(1, 2)
    exchange(0)
    for cp in locals_:
        cp.wait()
    forward(2, 0)
    forward(2, 1)
    forward(2, 2)
    send(1, 3)
    exchange(1)
    units((0,), 0, 1, 4, 2, 5)
    exchange(2)
    exchange(3)
    forward(3, 0)
    forward(3, 1)
    forward(3, 2)
    forward(1, 3)
    units((1,), 0, 1, 4, 2, 5)
    units((0, 1), 3, 6)
    ex[0].wait_recv()
    ex[1].wait_recv()
    send(1, 4)
    units((2,), 0, 1, 4, 2, 5, 3, 6)
    ex[2].wait_recv()
    ex[3].wait_recv()
    units((3,), 0, 1, 4, 2, 5, 3, 6)
    hop(0, 4, 0).wait_recv()
    hop(1, 4, 1).wait_recv()
    forward(2, 3)
    send(1, 5)
    units((3, 1, 2, 0), 7)

    order = [(j, i) for j in range(PARTS) for i in (1, 0)]

    def down(k, j):
        return dot_nt(act[pl.ds(k * HALF_ROWS, HALF_ROWS)], wd[pl.ds(j * FEAT, FEAT)])

    def part_of(ref, j, i):
        return ref.at[j, pl.ds(i * HALF_ROWS, HALF_ROWS)]

    px = [
        remote(part_of(ps, j, i), part_of(pr, j, i), px_s.at[n], px_r.at[n], pair, s)
        for n, (j, i) in enumerate(order)
    ]
    near = lax.rem(h + NH - 1 + 2 * lo, NH)

    def give(j, i):
        r = pl.ds(i * HALF_ROWS, HALF_ROWS)
        bs[j, r] = (mine[j, r] + pr[j, r].astype(F32)).astype(BF16)

        def back(n, _, kinds=(3, 1, 2, 0)):
            dx, tc = 2 * i + n // NC, lax.rem(c + lax.rem(n, NC), NC)
            for kind in kinds:
                to_h = (h, near, near, lax.rem(h + 2, NH))[kind]
                to_lo = (lo, 0, 1, 1 - lo)[kind]
                t = (lax.rem(x + NX - dx, NX) * NH + to_h) * NC + tc
                remote(
                    bs.at[j, pl.ds(place(dx, kind, tc), CAP)],
                    bk.at[j, pl.ds(aligned(s * CAP), CAP)],
                    ret_s.at[j], ret_r.at[j], to_lo * NY + y, t,
                ).start()
            return 0

        if i == 0:
            back(0, 0, kinds=(3, 1, 2))
            bk[j, pl.ds(aligned(s * CAP), CAP)] = bs[j, pl.ds(place(0, 0, c), CAP)]
        lax.fori_loop(1 if i == 0 else 0, 2 * NC, back, 0)

    def arrived(a):
        for way in range(2):
            hop(way, 4, a).wait_recv()

    passing = {0: ((3, 3), (1, 4)), 1: ((2, 4), (1, 5)), 2: ((3, 4), (2, 5)), 3: ((3, 5),)}
    for n, (j, i) in enumerate(order):
        waits = n % 2 == 0
        if n >= AHEAD and waits:
            px[n - AHEAD].wait_recv()
            give(*order[n - AHEAD])
        if waits:
            arrived(2 + j * BLOCKS // PARTS)
        r = pl.ds(i * HALF_ROWS, HALF_ROWS)
        ps[j, r] = down(2 + i, j).astype(BF16)
        if n >= AHEAD and not waits:
            px[n - AHEAD].wait_recv()
        px[n].start()
        if n >= AHEAD and not waits:
            give(*order[n - AHEAD])
        mine[j, r] = down(i, j)
        for step, a in passing.get(n, ()):
            forward(step, a)
    for n in range(len(order) - AHEAD, len(order)):
        px[n].wait_recv()
        give(*order[n])

    for j in range(PARTS):
        block = bk.at[j, pl.ds(0, SLOTS - CAP)]
        remote(block, block, ret_s.at[j], ret_r.at[j], b, s).wait_recv()
        cols = pl.ds(j * FEAT, FEAT)
        out[0, :, cols] = (mixed[:, cols] + gate_s[...] * dot(sel[...], bk[j])).astype(BF16)

    tail.wait_send()
    head.wait_send()
    for cp in hops + ex + px:
        cp.wait_send()
    block = packed.at[pl.ds(0, SLOTS - CAP)]
    remote(block, block, fwd_s, fwd_r.at[0], b, s).wait_send()
    for j in range(PARTS):
        block = bs.at[j, pl.ds(0, SLOTS - CAP)]
        remote(block, block, ret_s.at[j], ret_r.at[j], b, s).wait_send()


def on_device(tokens, expert_ids, expert_capacity, kernel_weight, norm_gain, router, expert_gate, expert_up, expert_down):
    dma = pltpu.SemaphoreType.DMA
    vmem = pl.BlockSpec(memory_space=pltpu.VMEM)
    anywhere = pl.BlockSpec(memory_space=pl.ANY)
    return pl.pallas_call(
        layer,
        out_shape=jax.ShapeDtypeStruct((1, TOK, D), BF16),
        in_specs=[anywhere, vmem, vmem, anywhere, vmem, vmem] + [anywhere] * 3,
        out_specs=vmem,
        scratch_shapes=[
            pltpu.VMEM((TOK + 4 * CAP, D), BF16),
            pltpu.VMEM((HEADS * TAPS, D), BF16),
            pltpu.VMEM((4, TOK, 128), F32),
            pltpu.VMEM((TOK, D), F32),
            pltpu.VMEM((TOK, D), BF16),
            pltpu.VMEM((SLOTS, D), BF16),
            pltpu.VMEM((TOK, SLOTS), BF16),
            pltpu.VMEM((TOK, 1), F32),
            pltpu.VMEM((2 * SLOTS, D), BF16),
            pltpu.VMEM((NY, D, 2 * PIECE), BF16),
            pltpu.VMEM((D, NY * PIECE), BF16),
            pltpu.VMEM((2 * SLOTS, NY * PIECE), BF16),
            pltpu.VMEM((PARTS, SLOTS, FEAT), BF16),
            pltpu.VMEM((PARTS, SLOTS, FEAT), BF16),
            pltpu.VMEM((PARTS, SLOTS, FEAT), F32),
            pltpu.VMEM((PARTS, SLOTS, FEAT), BF16),
            pltpu.VMEM((PARTS, SLOTS, FEAT), BF16),
            dma((2,)),
            dma((2 + BLOCKS,)),
            dma((2,)), dma((2,)),
            dma((2, 4, 2 + BLOCKS)), dma((2, 4, 2 + BLOCKS)),
            dma, dma((4,)),
            dma((4,)), dma((4,)),
            dma((2 * PARTS,)), dma((2 * PARTS,)),
            dma((PARTS,)), dma((PARTS,)),
        ],
        compiler_params=pltpu.CompilerParams(
            collective_id=0, has_side_effects=True, vmem_limit_bytes=56 * 1024 * 1024
        ),
    )(
        tokens,
        expert_ids.reshape(1, TOK),
        expert_capacity.reshape(1, EXPERTS),
        kernel_weight.T,
        norm_gain,
        router.T,
        expert_gate,
        expert_up,
        expert_down,
    )


def solution(mesh):
    placed = (
        P("blk", "seq", None),
        P("blk", "seq", None),
        P(),
        P(),
        P(),
        P(),
        P("seq", None, "blk"),
        P("seq", None, "blk"),
        P("seq", None, "blk"),
    )
    return jax.shard_map(
        on_device, mesh=mesh, in_specs=placed, out_specs=P("blk", "seq", None), check_vma=False
    )
```
